256 devices in a mesh: body: 8 (over z), gx: 8 (over y, core), gy: 4 (over x).
Axes of the slice: x: 4, y: 4, z: 8, core: 2. Of those that a mesh axis runs over, the one named last changes fastest.
Arguments:
- load: float32 [128, 512, 512], P('body', 'gx', 'gy'), may hold values from -8 to 8
- stiffness: float32 [128, 512, 512], P('body', 'gx', 'gy'), may hold values from 0.1 to 3
- pair_code: int32 [4, 512, 512], P(None, 'gx', 'gy'), may hold values from 0 to 24
- pair_weight: float32 [4, 512, 512], P(None, 'gx', 'gy'), may hold values from 0.05 to 0.5
Outputs:
- solution: float32 [128, 512, 512], P('body', 'gx', 'gy')
- interface_load: float32 [128, 512, 512], P('body', 'gx', 'gy')
The draws below stay inside these ranges and needn't reach their ends.
Inputs may be any that keep to these rules, and one draw needn't show every extreme that they name: `pair_code`: entry k of slave node (i, j) ties it to the master node (i + c // 5 - 2, j + c % 5 - 2) of the top layer of the body below, c being the entry; the same pairing holds at every interface; masters outside the grid count as zero.
All inputs are finite; a program needn't handle non-finite values.
Results may differ from the reference program's by a relative error of at most 0.0001.
Values sent between devices are 32-bit elements; how exact they have to be, the bound alone decides.
A program may use at most 64 MiB of HBM per device.

```python
import math
import jax
import jax.numpy as jnp

CZ = 16
REACH = 2
PAIRS = 4
UZAWA = 2
INNER = 3
NZ = 128
NX = 512
NY = 512


def plant(result, rng, smallest, largest):
    shape = result.shape
    place = [jax.random.randint(jax.random.fold_in(rng, axis), (), 0, shape[axis]) for axis in range(len(shape))]
    result = result.at[tuple(place)].set(smallest)
    longest = shape.index(max(shape))
    place[longest] = (place[longest] + 1) % shape[longest]
    return result.at[tuple(place)].set(largest)


def shard_levels(own_key, extent, split, smallest, top_value):
    def one(axis_at, parts):
        steps = jax.random.uniform(jax.random.fold_in(jax.random.fold_in(own_key, 6), axis_at), (parts,), jnp.float32, smallest / len(split), top_value / len(split))
        return jnp.repeat(jnp.exp(steps), extent[axis_at] // parts).reshape((-1,) + (1,) * (len(extent) - axis_at - 1))

    level = one(*split[0])
    for cut in split[1:]:
        level = level * one(*cut)
    return level


def scatter_about(key, dims, scale, bound, pieces=(), dtype=jnp.bfloat16):
    array = jax.random.normal(key, dims, jnp.float32) * scale
    if len(pieces) > 0:
        array = shard_levels(key, dims, pieces, -0.22, 0.18) * array
    return jnp.clip(array, min=-bound, max=bound).astype(dtype)


def setup_inputs(seed: int = 0) -> dict:
    keys = jax.random.split(jax.random.key(seed), 5)
    return {
        "load": scatter_about(keys[0], (NZ, NX, NY), 1.0, 8.0, ((0, 8), (1, 8), (2, 4)), jnp.float32),
        "stiffness": jnp.clip(jnp.exp(math.log(3.0) - 3.4011974 * jax.random.uniform(keys[1], (NZ, NX, NY), jnp.float32) ** shard_levels(keys[1], (NZ, NX, NY), ((0, 8), (1, 8), (2, 4)), -0.2, 0.2)), 0.1, 3.0),
        "pair_code": plant(jax.random.randint(keys[2], (PAIRS, NX, NY), 0, (2 * REACH + 1) ** 2), jax.random.fold_in(keys[2], 1), 0, ((2 * REACH + 1) ** 2) - 1).astype(jnp.int32),
        "pair_weight": jnp.clip(0.05 + 0.45 * jax.random.uniform(keys[3], (PAIRS, NX, NY), jnp.float32) ** shard_levels(keys[3], (PAIRS, NX, NY), ((1, 8), (2, 4)), -0.2, 0.2), 0.05, 0.5),
    }


RATE = 2.0


def apply_operator(vector, stiffness):
    padded = jnp.pad(vector, 1)
    layer_index = jnp.arange(vector.shape[0])[:, None, None]
    upper_term = jnp.where(layer_index % CZ == CZ - 1, 0.0, padded[2:, 1:-1, 1:-1])
    lower_term = jnp.where(layer_index % CZ == 0, 0.0, padded[:-2, 1:-1, 1:-1])
    beside = upper_term + lower_term + padded[1:-1, 2:, 1:-1] + padded[1:-1, :-2, 1:-1]
    beside = beside + padded[1:-1, 1:-1, 2:] + padded[1:-1, 1:-1, :-2]
    return (6.0 + stiffness) * vector - beside


def body_sums(first, second):
    bodies = first.shape[0] // CZ
    product = (first * second).reshape(bodies, CZ, -1)
    sums = jnp.sum(product, axis=(1, 2))
    return jnp.repeat(sums, CZ)[:, None, None]


def offset_table(codes, weights):
    offset_span = 2 * REACH + 1
    tables = []
    for offset in range(offset_span * offset_span):
        tables.append(jnp.sum(jnp.where(codes == offset, weights, 0.0), axis=0))
    return tables


def reference(load, stiffness, pair_code, pair_weight):
    offset_span = 2 * REACH + 1
    layers = load.shape[0]
    bodies = layers // CZ
    face_rows = load.shape[1]
    face_cols = load.shape[2]
    tables = offset_table(pair_code, pair_weight)
    multiplier = jnp.zeros((bodies - 1, face_rows, face_cols), jnp.float32)
    solution = jnp.zeros_like(load)
    interface_load = jnp.zeros_like(load)
    for outer_step in range(UZAWA):
        residual = load + interface_load - apply_operator(solution, stiffness)
        direction = residual
        norm_now = body_sums(residual, residual)
        for inner_step in range(INNER):
            image = apply_operator(direction, stiffness)
            alpha = norm_now / body_sums(direction, image)
            solution = solution + alpha * direction
            residual = residual - alpha * image
            norm_next = body_sums(residual, residual)
            direction = residual + (norm_next / norm_now) * direction
            norm_now = norm_next
        stacked = solution.reshape(bodies, CZ, face_rows, face_cols)
        master = jnp.pad(stacked[:-1, CZ - 1], ((0, 0), (REACH, REACH), (REACH, REACH)))
        slave = stacked[1:, 0]
        pulled = jnp.zeros_like(slave)
        for offset in range(offset_span * offset_span):
            shift_row = offset // offset_span - REACH
            shift_col = offset % offset_span - REACH
            window = master[:, REACH + shift_row:REACH + shift_row + face_rows, REACH + shift_col:REACH + shift_col + face_cols]
            pulled = pulled + tables[offset][None] * window
        multiplier = multiplier + RATE * (slave - pulled)
        force = jnp.zeros_like(slave)
        for offset in range(offset_span * offset_span):
            shift_row = offset // offset_span - REACH
            shift_col = offset % offset_span - REACH
            spread = jnp.pad(tables[offset][None] * multiplier, ((0, 0), (REACH, REACH), (REACH, REACH)))
            force = force + spread[:, REACH - shift_row:REACH - shift_row + face_rows, REACH - shift_col:REACH - shift_col + face_cols]
        shaped = jnp.zeros((bodies, CZ, face_rows, face_cols), jnp.float32)
        shaped = shaped.at[:-1, CZ - 1].set(force).at[1:, 0].set(-multiplier)
        interface_load = shaped.reshape(layers, face_rows, face_cols)
    return solution, interface_load
```

```python
import functools

import jax
import jax.numpy as jnp
from jax import lax
from jax.experimental import pallas as pl
from jax.experimental.pallas import tpu as pltpu
from jax.sharding import PartitionSpec as P

MESH = pl.DeviceIdType.MESH
F32 = jnp.float32

NBODY, NGX, NGY = 8, 8, 4
NPEER = NGX * NGY
CZ, BR, BC = 16, 64, 128
REACH, SPAN, RATE = 2, 5, 2.0
OFF = 24
ROWS = BR + 2 * OFF
LO, HI = 8, ROWS - 8
NLO, NHI = 16, ROWS - 16
W = 12
SLOTS = 10
SHIFT = 6.0


def roll(x, by):
    by %= BC
    return x if by == 0 else pltpu.roll(x, by, x.ndim - 1)


def lanes(shape):
    return lax.broadcasted_iota(jnp.int32, shape, len(shape) - 1)


def moved(a, b, by):
    if by == 0:
        return a, b
    lane = lanes(a.shape)
    late = lane < by if by > 0 else lane >= BC + by
    return roll(jnp.where(late, b, a), -by), roll(jnp.where(late, a, b), -by)


def chunks(first, last, step):
    return [(r, min(step, last - r)) for r in range(first, last, step)]


def kernel(
    load, stiff, code, weight, sol, ifl,
    va, vb, ua, ub, sa, sb, ci, ca, cb, wa, wb, sl, sr, pl_, pr, ta, tb,
    sha, shb, fa, fb, ma, mb, stage, fdn, fup, gdn, gup, mrow, mbuf, mz,
    lsem, rs, rr, fs, fr, gs, gr, as_, ar, zs, zr,
):
    body, gx, gy = (lax.axis_index(n) for n in ("body", "gx", "gy"))
    me = gx * NGY + gy
    gxm, gxp = lax.rem(gx + NGX - 1, NGX), lax.rem(gx + 1, NGX)
    gym, gyp = lax.rem(gy + NGY - 1, NGY), lax.rem(gy + 1, NGY)
    below, above = lax.rem(body + NBODY - 1, NBODY), lax.rem(body + 1, NBODY)

    def peer(o):
        p = lax.rem(me + o, NPEER)
        return (body, p // NGY, lax.rem(p, NGY))

    barrier = pltpu.get_barrier_semaphore()

    def greet(o, carry):
        pl.semaphore_signal(barrier, inc=1, device_id=peer(o), device_id_type=MESH)
        return carry

    locals_ = [
        pltpu.make_async_copy(load, va.at[0, pl.ds(1, CZ), pl.ds(OFF, BR), :], lsem.at[0]),
        pltpu.make_async_copy(stiff, sa.at[:, pl.ds(OFF, BR), :], lsem.at[1]),
        pltpu.make_async_copy(code, ci.at[:, pl.ds(OFF, BR), :], lsem.at[2]),
        pltpu.make_async_copy(weight, wa.at[:, pl.ds(OFF, BR), :], lsem.at[3]),
    ]
    for c in locals_:
        c.start()
    lax.fori_loop(1, NPEER, greet, 0)
    pl.semaphore_signal(barrier, inc=1, device_id=(below, gx, gy), device_id_type=MESH)
    pl.semaphore_signal(barrier, inc=1, device_id=(above, gx, gy), device_id_type=MESH)

    one = jnp.float32(1.0)
    zero = jnp.float32(0.0)
    top_ok = jnp.where(gx > 0, one, zero)
    bot_ok = jnp.where(gx < NGX - 1, one, zero)
    right_ok = jnp.where(gy < NGY - 1, one, zero)
    left_ok = jnp.where(gy > 0, one, zero)
    up_ok = jnp.where(body < NBODY - 1, one, zero)
    dn_ok = jnp.where(body > 0, one, zero)

    zl = jnp.zeros((ROWS, BC), F32)
    for k in range(4):
        for l in (0, CZ + 1):
            va[k, l] = zl
            vb[k, l] = zl
            if k < 3:
                ua[k, l] = zl
                ub[k, l] = zl
    z8 = jnp.zeros((8, BC), F32)
    for l in range(2, 13):
        for r in (LO, NHI):
            va[0, 1 + l, r : r + 8] = z8
            sa[l, r : r + 8] = z8
    for k in range(4):
        for r in (LO, NHI):
            wa[k, r : r + 8] = z8

    for c in locals_:
        c.wait()

    def item(q, r):
        if q < CZ:
            return va[0, 1 + q, pl.ds(r, 8), :]
        if q < 2 * CZ:
            return sa[q - CZ, pl.ds(r, 8), :]
        if q < 2 * CZ + 4:
            return ci[q - 2 * CZ, pl.ds(r, 8), :].astype(F32)
        return wa[q - 2 * CZ - 4, pl.ds(r, 8), :]

    lane8 = lanes((8, BC))

    def pack(t, carry):
        o = pl.multiple_of(8 * t, 8)
        r = pl.multiple_of(8 * t + OFF, 8)
        for j in range(4):
            left = right = None
            for s in range(SLOTS):
                x = item(SLOTS * j + s, r)
                xl, xr = roll(x, W * s), roll(x, W * s + W)
                left = xl if s == 0 else jnp.where(lane8 >= W * s, xl, left)
                right = xr if s == 0 else jnp.where(lane8 >= W * s, xr, right)
            sl[j, pl.ds(o, 8), :] = left
            sr[j, pl.ds(o, 8), :] = right
        return carry

    lax.fori_loop(0, BR // 8, pack, 0)

    pl.semaphore_wait(barrier, NPEER - 1 + 2)

    sends = []

    def send(src, dst, dev):
        n = len(sends)
        c = pltpu.make_async_remote_copy(src, dst, rs.at[n], rr.at[n], device_id=dev, device_id_type=MESH)
        c.start()
        sends.append(c)

    def column_sends(buf, dst, dev_y):
        send(buf.at[:, pl.ds(0, BR), :], dst.at[:, pl.ds(OFF, BR), :], (body, gx, dev_y))

    def corner_sends(buf, dst, dev_y):
        send(buf.at[:, pl.ds(0, 16), :], dst.at[:, pl.ds(OFF + BR, 16), :], (body, gxm, dev_y))
        send(buf.at[:, pl.ds(BR - 16, 16), :], dst.at[:, pl.ds(LO, 16), :], (body, gxp, dev_y))

    column_sends(sl, pr, gym)
    column_sends(sr, pl_, gyp)
    for dev, near, to_near, far, to_far in (
        ((body, gxm, gy), OFF, OFF + BR, OFF + 8, OFF + BR + 8),
        ((body, gxp, gy), OFF + BR - 8, NLO, OFF + BR - 16, LO),
    ):
        for ref, lead in ((va, (0,)), (sa, ())):
            base = 1 if lead else 0

            def part(l, n, r):
                return ref.at[lead + (pl.ds(base + l, n), pl.ds(r, 8), slice(None))]

            send(part(0, CZ, near), part(0, CZ, to_near), dev)
            send(part(0, 2, far), part(0, 2, to_far), dev)
            send(part(13, 3, far), part(13, 3, to_far), dev)
        send(ci.at[:, pl.ds(near, 8), :], ci.at[:, pl.ds(to_near, 8), :], dev)
        send(wa.at[:, pl.ds(near, 8), :], wa.at[:, pl.ds(to_near, 8), :], dev)
    corner_sends(sl, pr, gym)
    corner_sends(sr, pl_, gyp)
    for c in sends:
        c.wait_recv()

    right_lane = lane8 < W
    left_lane = lane8 >= BC - W
    lane_ok = jnp.where(lane8 < BC // 2, right_ok, left_ok)

    def unpack(t, carry):
        r = pl.multiple_of(8 * t + LO, 8)
        row_ok = jnp.where(t < 2, top_ok, jnp.where(t >= 10, bot_ok, one))
        ok = lane_ok * row_ok
        for j in range(4):
            x_r = pr[j, pl.ds(r, 8), :]
            x_l = pl_[j, pl.ds(r, 8), :]
            for s in range(SLOTS):
                q = SLOTS * j + s
                x = jnp.where(right_lane, roll(x_r, -W * s), jnp.where(left_lane, roll(x_l, -W - W * s), 0.0))
                if q < CZ:
                    vb[0, 1 + q, pl.ds(r, 8), :] = x * ok
                elif q < 2 * CZ:
                    sb[q - CZ, pl.ds(r, 8), :] = x
                elif q < 2 * CZ + 4:
                    cb[q - 2 * CZ, pl.ds(r, 8), :] = x
                else:
                    wb[q - 2 * CZ - 4, pl.ds(r, 8), :] = x * ok
        return carry

    lax.fori_loop(0, (HI - LO) // 8, unpack, 0)

    def mask_rows(l, carry):
        va[0, l, LO:OFF] = va[0, l, LO:OFF] * top_ok
        va[0, l, OFF + BR : HI] = va[0, l, OFF + BR : HI] * bot_ok
        return carry

    lax.fori_loop(1, CZ + 1, mask_rows, 0)
    for k in range(4):
        wa[k, NLO:OFF] = wa[k, NLO:OFF] * top_ok
        wa[k, OFF + BR : NHI] = wa[k, OFF + BR : NHI] * bot_ok
        ca[k, NLO:NHI] = ci[k, NLO:NHI].astype(F32)

    step = 16
    lane16 = lanes((step, BC))
    first, last = lane16 == 0, lane16 == BC - 1
    lane_ok16 = jnp.where(lane16 < BC // 2, right_ok, left_ok)

    def row_ok_of(r):
        return top_ok if r < OFF else bot_ok if r >= OFF + BR else None

    def segments(lo, hi):
        return chunks(lo, OFF, step) + chunks(OFF, OFF + BR, step) + chunks(OFF + BR, hi, step)

    def fold(x):
        return jnp.sum(x.reshape(x.shape[0] // 8, 8, BC), axis=0)

    def apply(sa_ref, sb_ref, k, da_ref, db_ref, kd, lo, hi, beside=True):
        def layer(l, acc):
            acc0, acc1 = acc
            for r, n in segments(lo, hi):
                rows = slice(r, r + n)
                a, b = sa_ref[k, l, rows], sb_ref[k, l, rows]
                f, e = first[:n], last[:n]
                near = roll(jnp.where(e, b, a), 1) + roll(jnp.where(f, b, a), -1)
                near = near + (sa_ref[k, l, r - 1 : r - 1 + n] + sa_ref[k, l, r + 1 : r + 1 + n])
                near = near + (sa_ref[k, l - 1, rows] + sa_ref[k, l + 1, rows])
                out = sa[l - 1, rows] * a - near
                ok = row_ok_of(r)
                if ok is not None:
                    out = out * ok
                else:
                    acc0 = acc0 + fold(a * a)
                    acc1 = acc1 + fold(a * out)
                if da_ref is not None:
                    da_ref[kd, l, rows] = out
                if beside:
                    near = roll(jnp.where(e, a, b), 1) + roll(jnp.where(f, a, b), -1)
                    near = near + (sb_ref[k, l, r - 1 : r - 1 + n] + sb_ref[k, l, r + 1 : r + 1 + n])
                    near = near + (sb_ref[k, l - 1, rows] + sb_ref[k, l + 1, rows])
                    out = sb[l - 1, rows] * b - near
                    okb = lane_ok16[:n] if ok is None else lane_ok16[:n] * ok
                    db_ref[kd, l, rows] = out * okb
            return acc0, acc1

        z = jnp.zeros((8, BC), F32)
        return lax.fori_loop(1, CZ + 1, layer, (z, z))

    row_lane = lanes((1, BC))

    def send_sums(n, accs):
        row = jnp.zeros((1, BC), F32)
        for k, acc in enumerate(accs):
            row = row + jnp.where(row_lane == k, jnp.sum(acc, keepdims=True), 0.0)
        mrow[n, 0] = row
        mbuf[n, me] = row

        def go(o, carry):
            pltpu.make_async_remote_copy(
                mrow.at[n, 0], mbuf.at[n, me], as_.at[n], ar.at[n], device_id=peer(o), device_id_type=MESH
            ).start()
            return carry

        lax.fori_loop(1, NPEER, go, 0)

    def others(n):
        return mbuf.at[n, pl.ds(0, NPEER - 1)]

    def total_sums(n):
        pltpu.make_async_copy(others(n), others(n), ar.at[n]).wait()
        total = jnp.sum(mbuf[n], axis=0)
        mz[n, 2] = total
        for side, dev in ((0, above), (1, below)):
            pltpu.make_async_remote_copy(
                mz.at[n, 2], mz.at[n, side], zs.at[n, side], zr.at[n, side],
                device_id=(dev, gx, gy), device_id_type=MESH,
            ).start()
        return total

    def wait_z(n):
        for side, dev in ((0, above), (1, below)):
            pltpu.make_async_remote_copy(
                mz.at[n, 2], mz.at[n, side], zs.at[n, side], zr.at[n, side],
                device_id=(dev, gx, gy), device_id_type=MESH,
            ).wait()

    def coefficients(total):
        m = [jnp.sum(jnp.where(row_lane == k, total, 0.0), axis=1, keepdims=True) for k in range(6)]
        h = [m[k + 1] + SHIFT * m[k] for k in range(5)]
        l10, l20 = h[1] / h[0], h[2] / h[0]
        d1 = h[2] - l10 * h[1]
        e12 = h[3] - l20 * h[1]
        l21 = e12 / d1
        d2 = h[4] - l20 * h[2] - l21 * e12
        y1 = m[1] - l10 * m[0]
        y2 = m[2] - l20 * m[0] - l21 * y1
        c2 = y2 / d2
        c1 = y1 / d1 - l21 * c2
        c0 = m[0] / h[0] - l10 * c1 - l20 * c2
        return [jnp.broadcast_to(c, (step, BC)) for c in (c0, c1, c2)]

    fsends = []

    def send_faces(n, a_ref, b_ref, dn, up, sem_s, sem_r):
        out = []
        for side, (l, dst, dev) in enumerate(((1, dn, below), (CZ, up, above))):
            for r, cnt in chunks(NLO, NHI, step):
                lane = lane16[:cnt]
                x = b_ref[0, l, r : r + cnt]
                for k in (1, 2):
                    mine = (lane >= 2 * W * k - W) & (lane < 2 * W * k + W)
                    x = jnp.where(mine, roll(b_ref[k, l, r : r + cnt], 2 * W * k), x)
                stage[n, side, r - NLO : r - NLO + cnt] = x
            for k in range(4):
                src = stage.at[n, side] if k == 3 else a_ref.at[k, l, pl.ds(NLO, NHI - NLO), :]
                c = pltpu.make_async_remote_copy(
                    src, dst.at[k], sem_s.at[4 * side + k], sem_r.at[4 * side + k],
                    device_id=(dev, gx, gy), device_id_type=MESH,
                )
                c.start()
                out.append(c)
        return out

    def received(ref, c, r, n):
        at = slice(r - NLO, r - NLO + n)
        x = [c[k][:n] * ref[k, at] for k in range(3)]
        packed = ref[3, at]
        y = [c[k][:n] * roll(packed, -2 * W * k) for k in range(3)]
        return x[0] + x[1] + x[2], y[0] + y[1] + y[2]

    def pull(lo, hi, beside):
        for r, n in chunks(lo - 8, hi + 8, step):
            a, b = fa[r : r + n], fb[r : r + n]
            for d in range(SPAN):
                x, y = moved(a, b, d - REACH)
                sha[d, r : r + n] = x
                if beside:
                    shb[d, r : r + n] = y
        for r, n in chunks(lo, hi, step):
            x = y = jnp.zeros((n, BC), F32)
            for c in range(SPAN * SPAN):
                dx, d = c // SPAN - REACH, c % SPAN
                x = x + ta[c, r : r + n] * sha[d, r + dx : r + dx + n]
                if beside:
                    y = y + tb[c, r : r + n] * shb[d, r + dx : r + dx + n]
            yield r, n, x, y

    def push(lo, hi, beside):
        for r, n in chunks(lo, hi, step):
            x = y = jnp.zeros((n, BC), F32)
            for d in range(SPAN):
                p = q = jnp.zeros((n, BC), F32)
                for dx in range(-REACH, REACH + 1):
                    c = (dx + REACH) * SPAN + d
                    p = p + ta[c, r - dx : r - dx + n] * ma[r - dx : r - dx + n]
                    q = q + tb[c, r - dx : r - dx + n] * mb[r - dx : r - dx + n]
                p, q = moved(p, q, REACH - d)
                x, y = x + p, y + q
            if beside:
                ok = lane_ok16[:n]
                row_ok = row_ok_of(r) if n == 8 else None
                if row_ok is not None:
                    x, ok = x * row_ok, ok * row_ok
                y = y * ok
            yield r, n, x, y

    s01 = apply(va, vb, 0, va, vb, 1, LO, HI)
    s23 = apply(va, vb, 1, va, vb, 2, LO, HI)
    faces = send_faces(0, va, vb, fdn, fup, fs, fr)
    s45 = apply(va, vb, 2, va, vb, 3, NLO, NHI)
    send_sums(0, s01 + s23 + s45)

    def tables(c, carry):
        code_at = c.astype(F32)
        for r, n in chunks(NLO, NHI, step):
            rows = slice(r, r + n)
            x = y = jnp.zeros((n, BC), F32)
            for k in range(4):
                x = x + jnp.where(ca[k, rows] == code_at, wa[k, rows], 0.0)
                y = y + jnp.where(cb[k, rows] == code_at, wb[k, rows], 0.0)
            ta[c, rows] = x
            tb[c, rows] = y
        return carry

    lax.fori_loop(0, SPAN * SPAN, tables, 0)

    co = coefficients(total_sums(0))
    g = [1.0 - SHIFT * co[0], -(co[0] + SHIFT * co[1]), -(co[1] + SHIFT * co[2]), -co[2]]

    def residual(l, carry):
        for r, n in chunks(NLO, NHI, step):
            rows = slice(r, r + n)
            ua[0, l, rows] = (g[0][:n] * va[0, l, rows] + g[1][:n] * va[1, l, rows]) + (
                g[2][:n] * va[2, l, rows] + g[3][:n] * va[3, l, rows]
            )
            ub[0, l, rows] = (g[0][:n] * vb[0, l, rows] + g[1][:n] * vb[1, l, rows]) + (
                g[2][:n] * vb[2, l, rows] + g[3][:n] * vb[3, l, rows]
            )
        return carry

    lax.fori_loop(1, CZ + 1, residual, 0)

    wait_z(0)
    for c in faces:
        c.wait()
    cm, cp = coefficients(mz[0, 0]), coefficients(mz[0, 1])

    def combine(refs, k3, l, rows, n):
        a = refs[0]
        return (k3[0][:n] * a[0, l, rows] + k3[1][:n] * a[1, l, rows]) + k3[2][:n] * a[2, l, rows]

    for r, n in chunks(LO, HI, step):
        rows = slice(r, r + n)
        fa[rows] = combine((va,), co, CZ, rows, n)
        fb[rows] = combine((vb,), co, CZ, rows, n)
    scale_up = RATE * up_ok
    for r, n, x, y in pull(NLO, NHI, True):
        p, q = received(fdn, cp, r, n)
        ma[r : r + n] = scale_up * (p - x)
        mb[r : r + n] = scale_up * (q - y)
    for edge in (LO, NHI):
        ma[edge : edge + 8] = z8
        mb[edge : edge + 8] = z8
    for r0, r1 in ((NLO, OFF), (OFF, OFF + BR), (OFF + BR, NHI)):
        for r, n, x, y in push(r0, r1, True):
            ua[0, CZ, r : r + n] = ua[0, CZ, r : r + n] + x
            ub[0, CZ, r : r + n] = ub[0, CZ, r : r + n] + y

    for r, n in chunks(NLO, NHI, step):
        x, y = received(fup, cm, r, n)
        fa[r : r + n] = x
        fb[r : r + n] = y
    scale_dn = RATE * dn_ok
    for edge in (LO, NHI):
        fa[edge : edge + 8] = z8
        fb[edge : edge + 8] = z8
    low = []
    for r, n, x, y in pull(NLO, NHI, True):
        rows = slice(r, r + n)
        x = scale_dn * (combine((va,), co, 1, rows, n) - x)
        y = scale_dn * (combine((vb,), co, 1, rows, n) - y)
        ua[0, 1, rows] = ua[0, 1, rows] - x
        ub[0, 1, rows] = ub[0, 1, rows] - y
        stage[0, 2, r - NLO : r - NLO + n] = x

    t01 = apply(ua, ub, 0, ua, ub, 1, NLO, NHI)
    t23 = apply(ua, ub, 1, ua, ub, 2, NLO, NHI)
    faces = send_faces(1, ua, ub, gdn, gup, gs, gr)
    t45 = apply(ua, ub, 2, None, None, 0, OFF, OFF + BR, beside=False)
    send_sums(1, t01 + t23 + t45)

    zc = jnp.zeros((step, BC), F32)

    def clear(l, carry):
        for r, n in chunks(0, BR, step):
            ifl[l, r : r + n] = zc
        return carry

    lax.fori_loop(1, CZ - 1, clear, 0)

    eo = coefficients(total_sums(1))

    def answer(l, carry):
        for r, n in chunks(OFF, OFF + BR, step):
            rows = slice(r, r + n)
            x = combine((va,), co, l, rows, n) + combine((ua,), eo, l, rows, n)
            sol[l - 1, r - OFF : r - OFF + n] = x
        return carry

    lax.fori_loop(1, CZ + 1, answer, 0)

    wait_z(1)
    for c in faces:
        c.wait()
    em, ep = coefficients(mz[1, 0]), coefficients(mz[1, 1])

    for r, n in chunks(NLO, NHI, step):
        rows = slice(r, r + n)
        fa[rows] = combine((ua,), eo, CZ, rows, n)
        fb[rows] = combine((ub,), eo, CZ, rows, n)
    for r, n, x, y in pull(NLO, NHI, True):
        p, q = received(gdn, ep, r, n)
        ma[r : r + n] = 2.0 * ma[r : r + n] + scale_up * (p - x)
        mb[r : r + n] = 2.0 * mb[r : r + n] + scale_up * (q - y)
    for r, n, x, y in push(OFF, OFF + BR, False):
        ifl[CZ - 1, r - OFF : r - OFF + n] = x

    for r, n in chunks(NLO, NHI, step):
        x, y = received(gup, em, r, n)
        fa[r : r + n] = x
        fb[r : r + n] = y
    for r, n, x, y in pull(OFF, OFF + BR, False):
        rows = slice(r, r + n)
        x = 2.0 * stage[0, 2, r - NLO : r - NLO + n] + scale_dn * (combine((ua,), eo, 1, rows, n) - x)
        ifl[0, r - OFF : r - OFF + n] = -x

    for c in sends:
        c.wait_send()
    for n in range(2):
        pltpu.make_async_copy(others(n), others(n), as_.at[n]).wait()


def per_device(load, stiffness, pair_code, pair_weight):
    field = lambda k: pltpu.VMEM((k, CZ + 2, ROWS, BC), F32)
    plane = lambda *lead: pltpu.VMEM((*lead, ROWS, BC), F32)
    near = lambda *lead: pltpu.VMEM((*lead, NHI - NLO, BC), F32)
    dma = pltpu.SemaphoreType.DMA
    nsend = 22
    scratch = [
        field(4), field(4), field(3), field(3), plane(CZ), plane(CZ),
        pltpu.VMEM((4, ROWS, BC), jnp.int32), plane(4), plane(4), plane(4), plane(4),
        pltpu.VMEM((4, BR, BC), F32), pltpu.VMEM((4, BR, BC), F32), plane(4), plane(4),
        plane(SPAN * SPAN), plane(SPAN * SPAN), plane(SPAN), plane(SPAN), plane(), plane(), plane(), plane(),
        near(2, 3), near(4), near(4), near(4), near(4),
        pltpu.VMEM((2, 1, 1, BC), F32), pltpu.VMEM((2, NPEER, 1, BC), F32), pltpu.VMEM((2, 3, 1, BC), F32),
        dma((4,)), dma((nsend,)), dma((nsend,)), dma((8,)), dma((8,)), dma((8,)), dma((8,)),
        dma((2,)), dma((2,)), dma((2, 2)), dma((2, 2)),
    ]
    out = jax.ShapeDtypeStruct((CZ, BR, BC), F32)
    return pl.pallas_call(
        kernel,
        out_shape=(out, out),
        in_specs=[pl.BlockSpec(memory_space=pl.ANY)] * 4,
        out_specs=[pl.BlockSpec(memory_space=pltpu.VMEM)] * 2,
        scratch_shapes=scratch,
        compiler_params=pltpu.CompilerParams(collective_id=0, has_side_effects=True),
        name="uzawa",
    )(load, stiffness, pair_code, pair_weight)


def solution(mesh):
    return jax.shard_map(
        per_device,
        mesh=mesh,
        in_specs=(
            P("body", "gx", "gy"),
            P("body", "gx", "gy"),
            P(None, "gx", "gy"),
            P(None, "gx", "gy"),
        ),
        out_specs=(P("body", "gx", "gy"), P("body", "gx", "gy")),
        check_vma=False,
    )
```

```python
import jax
import jax.numpy as jnp
from jax import lax
from jax.experimental import pallas as pl
from jax.experimental.pallas import tpu as pltpu
from jax.sharding import PartitionSpec as P

MESH = pl.DeviceIdType.MESH
F32 = jnp.float32

NBODY, NGX, NGY = 8, 8, 4
NPEER = NGX * NGY
CZ, BR, BC = 16, 64, 128
REACH, SPAN, RATE = 2, 5, 2.0
OFF = 24
ROWS = BR + 2 * OFF
LO, HI = 8, ROWS - 8
NLO, NHI = 16, ROWS - 16
SLOT, HALF = 32, 16
PER = BC // SLOT
TILES = CZ // PER
UNIT = 8
SHIFT = 6.0
STIFF, LOAD, PAIRS = 0, 1, 9


def turn(x, by):
    if isinstance(by, int):
        by %= BC
        return x if by == 0 else pltpu.roll(x, by, x.ndim - 1)
    return pltpu.roll(x, lax.rem(by + BC, BC), x.ndim - 1)


def when(flag):
    return lambda f: f() if flag else None


def chunks(first, last, step):
    return [(r, min(step, last - r)) for r in range(first, last, step)]


def kernel(
    load, stiff, code, weight, sol, ifl,
    fa, fp, ci, cb, sl, sr, ml, mr, far, ta, tb, sha, shb, face, side_face, mult, low, force,
    stage, stage_low, got, acc, co, mrow, mbuf, mz,
    lsem, rs, rr, fs, fr, as_, ar, zs, zr,
):
    body, gx, gy = (lax.axis_index(n) for n in ("body", "gx", "gy"))
    me = gx * NGY + gy
    gxm, gxp = lax.rem(gx + NGX - 1, NGX), lax.rem(gx + 1, NGX)
    gym, gyp = lax.rem(gy + NGY - 1, NGY), lax.rem(gy + 1, NGY)
    below, above = lax.rem(body + NBODY - 1, NBODY), lax.rem(body + 1, NBODY)

    def peer(i):
        o = i + 12
        o = jnp.where(o >= NPEER, o - (NPEER - 1), o)
        p = me + o
        p = jnp.where(p >= NPEER, p - NPEER, p)
        return (body, p // NGY, lax.rem(p, NGY))

    barrier = pltpu.get_barrier_semaphore()

    def greet(i, carry):
        pl.semaphore_signal(barrier, inc=1, device_id=peer(i), device_id_type=MESH)
        return carry

    lax.fori_loop(0, NPEER - 1, greet, 0)
    pl.semaphore_signal(barrier, inc=1, device_id=(below, gx, gy), device_id_type=MESH)
    pl.semaphore_signal(barrier, inc=1, device_id=(above, gx, gy), device_id_type=MESH)

    own_rows = pl.ds(OFF, BR)
    locals_ = [
        pltpu.make_async_copy(stiff, fa.at[STIFF, pl.ds(1, CZ), own_rows, :], lsem.at[0]),
        pltpu.make_async_copy(load, fa.at[LOAD, pl.ds(1, CZ), own_rows, :], lsem.at[1]),
        pltpu.make_async_copy(code, ci, lsem.at[2]),
        pltpu.make_async_copy(weight, fa.at[PAIRS, pl.ds(4, 4), own_rows, :], lsem.at[3]),
    ]
    for c in locals_:
        c.start()

    one = jnp.float32(1.0)
    zero = jnp.float32(0.0)
    top_ok = jnp.where(gx > 0, one, zero)
    bot_ok = jnp.where(gx < NGX - 1, one, zero)
    right_ok = jnp.where(gy < NGY - 1, one, zero)
    left_ok = jnp.where(gy > 0, one, zero)
    scale_up = jnp.where(body < NBODY - 1, jnp.float32(RATE), zero)
    scale_dn = jnp.where(body > 0, jnp.float32(RATE), zero)

    step = 16
    z16 = jnp.zeros((step, BC), F32)
    z8 = jnp.zeros((8, BC), F32)

    def zero_ends(i, carry):
        for r, n in chunks(0, ROWS, step):
            for l in (0, CZ + 1):
                fa[i + LOAD, l, r : r + n] = z16
            for t in (0, TILES + 1):
                fp[i + LOAD, t, r : r + n] = z16
        return carry

    def zero_far(l, carry):
        for r in (LO, NHI):
            for k in range(4):
                fa[k, l, r : r + 8] = z8
        return carry

    lax.fori_loop(0, 8, zero_ends, 0)
    lax.fori_loop(1, CZ + 1, zero_far, 0)
    for k in range(2):
        for r in (LO, NHI):
            mult[k, r : r + 8] = z8
            for t in range(TILES):
                fp[k, t + 1, r : r + 8] = z8
        for r, n in chunks(NLO, NHI, step):
            mult[k, r : r + n] = z16
    for r, n in chunks(NLO, NHI, step):
        low[r : r + n] = z16

    lane8 = lax.broadcasted_iota(jnp.int32, (8, BC), 1)
    top_tile = TILES - 1
    units = [(u // PER, u % PER) for u in range(16)]

    def put(tile, i, items, skip):
        left = right = None
        for u, (field, layer) in enumerate(items):
            x = fa[field, layer, pl.ds(pl.multiple_of(8 * i + OFF, 8), 8), :]
            x_l, x_r = turn(x, UNIT * u - skip), turn(x, UNIT * u + UNIT + skip)
            left = x_l if u == 0 else jnp.where(lane8 >= UNIT * u, x_l, left)
            right = x_r if u == 0 else jnp.where(lane8 >= UNIT * u, x_r, right)
        at = pl.ds(pl.multiple_of(8 * i, 8), 8)
        sl[tile, at, :] = left
        sr[tile, at, :] = right

    def pack_near(i, carry):
        for tile in (STIFF, LOAD):
            put(tile, i, [(tile, 1 + PER * t + s) for s, t in units], 0)
        return carry

    def pack_far(i, carry):
        put(2, i, [(t // 2, 1 + PER * top_tile * (t % 2) + s) for s, t in units], UNIT)
        put(3, i, [(PAIRS, k) for k in range(8)], 0)
        return carry

    for c in locals_:
        c.wait()
    lax.fori_loop(0, BR // 8, pack_near, 0)
    pl.semaphore_wait(barrier, NPEER - 1 + 2)

    count = [0]

    def send(src, dst, dev):
        n = count[0]
        count[0] += 1
        c = pltpu.make_async_remote_copy(src, dst, rs.at[n], rr.at[n], device_id=dev, device_id_type=MESH)
        c.start()
        return c

    near = []
    two = pl.ds(0, 2)
    ways = ((sl, mr, gym), (sr, ml, gyp))
    for buf, dst, dev_y in ways:
        near.append(send(buf.at[two], dst.at[two, own_rows, :], (body, gx, dev_y)))
    sides = (
        ((body, gxm, gy), OFF, OFF + BR, OFF + 8),
        ((body, gxp, gy), OFF + BR - 8, NLO, OFF + BR - 16),
    )
    layers = pl.ds(1, CZ)
    for dev, row, to, _ in sides:
        near.append(send(fa.at[two, layers, pl.ds(row, 8), :], fa.at[two, layers, pl.ds(to, 8), :], dev))
    for buf, dst, dev_y in ways:
        near.append(send(buf.at[two, pl.ds(0, 8), :], dst.at[two, pl.ds(OFF + BR, 8), :], (body, gxm, dev_y)))
        near.append(send(buf.at[two, pl.ds(BR - 8, 8), :], dst.at[two, pl.ds(NLO, 8), :], (body, gxp, dev_y)))

    for k in range(4):
        fa[PAIRS, k, OFF : OFF + BR] = ci[k].astype(F32)
    lax.fori_loop(0, BR // 8, pack_far, 0)
    late = []
    rest = pl.ds(2, 2)
    for buf, dst, dev_y in ways:
        late.append(send(buf.at[rest], dst.at[rest, own_rows, :], (body, gx, dev_y)))
        late.append(send(buf.at[rest, pl.ds(0, 16), :], dst.at[rest, pl.ds(OFF + BR, 16), :], (body, gxm, dev_y)))
        late.append(send(buf.at[rest, pl.ds(BR - 16, 16), :], dst.at[rest, pl.ds(LO, 16), :], (body, gxp, dev_y)))
        late.append(send(buf.at[two, pl.ds(8, 8), :], dst.at[two, pl.ds(NHI, 8), :], (body, gxm, dev_y)))
        late.append(send(buf.at[two, pl.ds(BR - 16, 8), :], dst.at[two, pl.ds(LO, 8), :], (body, gxp, dev_y)))
    pairs = pl.ds(0, 8)
    for side, (dev, row, to, far_row) in enumerate(sides):
        late.append(send(fa.at[two, layers, pl.ds(far_row, 8), :], far.at[side], dev))
        late.append(send(fa.at[PAIRS, pairs, pl.ds(row, 8), :], fa.at[PAIRS, pairs, pl.ds(to, 8), :], dev))

    def clear(l, carry):
        for r, n in chunks(0, BR, step):
            ifl[l, r : r + n] = z16
        return carry

    lax.fori_loop(1, CZ - 1, clear, 0)

    lane16 = lax.broadcasted_iota(jnp.int32, (step, BC), 1)
    first, last = lane16 == 0, lane16 == BC - 1
    lane_ok = jnp.where(lane16 < BC // 2, right_ok, left_ok)
    in_slot = lax.bitwise_and(lane16, SLOT - 1)
    slot_ok = jnp.where(in_slot < HALF, left_ok, right_ok)
    is_l0, is_r0 = in_slot == HALF - 1, in_slot == HALF
    near_l = (in_slot >= UNIT) & (in_slot < HALF)
    near_r = (in_slot >= HALF) & (in_slot < HALF + UNIT)
    far_l, far_r = in_slot < UNIT, in_slot >= SLOT - UNIT
    low_slot, high_slot = lane16 < SLOT, lane16 >= BC - SLOT

    def row_ok_of(r):
        return top_ok if r < OFF else bot_ok if r >= OFF + BR else None

    def segments(lo, hi):
        return chunks(lo, OFF, step) + chunks(OFF, OFF + BR, step) + chunks(OFF + BR, hi, step)

    def fold(x):
        return jnp.sum(x.reshape(x.shape[0] // 8, 8, BC), axis=0)

    def masked(x, r, n):
        ok = row_ok_of(r)
        x = x * slot_ok[:n]
        return x if ok is None else x * ok

    def columns(tile, t, r, n):
        rows = slice(r, r + n)
        x = jnp.where(near_r[:n], turn(mr[tile, rows], HALF - UNIT * t), 0.0)
        return jnp.where(near_l[:n], turn(ml[tile, rows], UNIT - UNIT * t), x)

    for c in near:
        c.wait_recv()

    def unpack(i, carry):
        tile, t = i // TILES, lax.rem(i, TILES)
        for r, n in segments(NLO, NHI):
            fp[tile, t + 1, r : r + n] = masked(columns(tile, t, r, n), r, n)
        return carry

    def mask_rows(l, carry):
        fa[LOAD, l, NLO:OFF] = fa[LOAD, l, NLO:OFF] * top_ok
        fa[LOAD, l, OFF + BR : NHI] = fa[LOAD, l, OFF + BR : NHI] * bot_ok
        return carry

    lax.fori_loop(0, 2 * TILES, unpack, 0)
    lax.fori_loop(1, CZ + 1, mask_rows, 0)

    def image_a(p, k, l, r, n):
        rows = slice(r, r + n)
        a = fa[k, l, rows]
        s = turn(jnp.where(last[:n], p, a), 1) + turn(jnp.where(first[:n], p, a), -1)
        s = s + (fa[k, l, r - 1 : r - 1 + n] + fa[k, l, r + 1 : r + 1 + n])
        s = s + (fa[k, l - 1, rows] + fa[k, l + 1, rows])
        out = fa[STIFF, l, rows] * a - s
        ok = row_ok_of(r)
        return a, out if ok is None else out * ok

    def image_p(own, k, t, r, n):
        edge = None
        for s in range(PER):
            x = turn(own[s], SLOT * s + HALF)
            edge = x if s == 0 else jnp.where(lane16[:n] >= SLOT * s, x, edge)
        rows = slice(r, r + n)
        p = fp[k, t + 1, rows]
        s = turn(jnp.where(is_l0[:n], edge, p), 1) + turn(jnp.where(is_r0[:n], edge, p), -1)
        s = s + (fp[k, t + 1, r - 1 : r - 1 + n] + fp[k, t + 1, r + 1 : r + 1 + n])
        s = s + turn(jnp.where(high_slot[:n], fp[k, t, rows], p), SLOT)
        s = s + turn(jnp.where(low_slot[:n], fp[k, t + 2, rows], p), -SLOT)
        return masked(fp[STIFF, t + 1, rows] * p - s, r, n)

    row_lane = lax.broadcasted_iota(jnp.int32, (1, BC), 1)

    def others(n):
        return mbuf.at[n, pl.ds(0, NPEER - 1)]

    def relays(n):
        return [
            pltpu.make_async_remote_copy(
                mz.at[n, 2], mz.at[n, side], zs.at[n, side], zr.at[n, side],
                device_id=(dev, gx, gy), device_id_type=MESH,
            )
            for side, dev in ((0, above), (1, below))
        ]

    def faces(n, which):
        k0 = pl.ds(LOAD + 4 * n, 3)

        def part(to, size):
            return fa.at[k0, 1, pl.ds(NLO + to, size), :], got.at[n, 0, pl.ds(0, 3), pl.ds(to, size), :]

        far_part = NHI - NLO - 8
        pairs_ = (
            (stage.at[n], got.at[n, 1], above),
            (*part(8, BR), below),
            (*part(0, 8), below),
            (*part(far_part, 8), below),
            (stage_low.at[n], got.at[n, 0, 3], below),
        )
        return [
            pltpu.make_async_remote_copy(
                x, y, fs.at[n, i], fr.at[n, i], device_id=(dev, gx, gy), device_id_type=MESH
            )
            for i, (x, y, dev) in enumerate(pairs_)
            if i in which
        ]

    def side_columns(k0, t, slot, r, cnt):
        x = None
        for k in range(3):
            y = turn(fp[k0 + k, t, r : r + cnt], SLOT * (k - slot))
            x = y if k == 0 else jnp.where(lane16[:cnt] >= SLOT * k, y, x)
        return x

    def send_early(n):
        k0 = LOAD + 4 * n
        for r, cnt in chunks(NLO, NHI, step):
            at = slice(r - NLO, r - NLO + cnt)
            for k in range(3):
                stage[n, k, at] = fa[k0 + k, CZ, r : r + cnt]
            stage[n, 3, at] = side_columns(k0, TILES, PER - 1, r, cnt)
        for c in faces(n, (0, 1)):
            c.start()

    def send_rest(n):
        k0 = LOAD + 4 * n
        for r, cnt in chunks(NLO, NHI, step):
            stage_low[n, r - NLO : r - NLO + cnt] = side_columns(k0, 1, 0, r, cnt)
        for c in faces(n, (2, 3, 4)):
            c.start()

    def coefficients(total, where):
        m = [jnp.sum(jnp.where(row_lane == k, total, 0.0), axis=1, keepdims=True) for k in range(6)]
        h = [m[k + 1] + SHIFT * m[k] for k in range(5)]
        inv = 1.0 / h[0]
        l10, l20 = h[1] * inv, h[2] * inv
        d1 = h[2] - l10 * h[1]
        e12 = h[3] - l20 * h[1]
        inv1 = 1.0 / d1
        l21 = e12 * inv1
        d2 = h[4] - l20 * h[2] - l21 * e12
        y1 = m[1] - l10 * m[0]
        y2 = m[2] - l20 * m[0] - l21 * y1
        c2 = y2 / d2
        c1 = y1 * inv1 - l21 * c2
        c0 = m[0] * inv - l10 * c1 - l20 * c2
        for k, c in enumerate((c0, c1, c2)):
            co[where, k] = jnp.broadcast_to(c, (step, BC))

    def combine(ref, k0, where, l, r, n):
        rows = slice(r, r + n)
        x = [co[where, k][:n] * ref[k0 + k, l, rows] for k in range(3)]
        return (x[0] + x[1]) + x[2]

    def moved(a, b, by):
        at = lane16[: a.shape[0]] - by
        late_ = (at < 0) | (at > BC - 1)
        return turn(jnp.where(late_, b, a), -by), turn(jnp.where(late_, a, b), -by)

    inner = chunks(NLO, NHI, step)
    nothing = tuple(jnp.zeros((n, BC), F32) for _, n in inner)

    def pull(side):
        def one(d, sums):
            xs, ys = sums
            for r, n in chunks(LO, HI, step):
                rows = slice(r, r + n)
                sha[rows], shb[rows] = moved(face[side, rows], side_face[side, rows], d - REACH)
            out_x, out_y = [], []
            for (r, n), x, y in zip(inner, xs, ys):
                for dx in range(SPAN):
                    c, q = dx * SPAN + d, r + dx - REACH
                    x = x + ta[c, r : r + n] * sha[q : q + n]
                    y = y + tb[c, r : r + n] * shb[q : q + n]
                out_x.append(x)
                out_y.append(y)
            return tuple(out_x), tuple(out_y)

        return lax.fori_loop(0, SPAN, one, (nothing, nothing))

    def push():
        def one(d, sums):
            xs, ys = sums
            out_x, out_y = [], []
            for (r, n), x, y in zip(inner, xs, ys):
                p = q = jnp.zeros((n, BC), F32)
                for dx in range(SPAN):
                    c, o = dx * SPAN + d, r - dx + REACH
                    p = p + ta[c, o : o + n] * mult[0, o : o + n]
                    q = q + tb[c, o : o + n] * mult[1, o : o + n]
                p, q = moved(p, q, REACH - d)
                out_x.append(x + p)
                out_y.append(y + q)
            return tuple(out_x), tuple(out_y)

        return lax.fori_loop(0, SPAN, one, (nothing, nothing))

    def far_tier():
        for c in late:
            c.wait_recv()

        def rows_in(l, carry):
            for side, (r, ok) in enumerate(((NHI, bot_ok), (LO, top_ok))):
                for k in range(2):
                    fa[k, l + 1, r : r + 8] = far[side, k, l] * ok
            return carry

        def columns_in(i, carry):
            tile, f = i // 2, lax.rem(i, 2)
            g = f + 2 * tile
            t = top_tile * f
            for r, n in segments(LO, HI):
                rows = slice(r, r + n)
                x = jnp.where(far_r[:n], turn(mr[2, rows], SLOT - UNIT - UNIT * g), columns(tile, t, r, n))
                x = jnp.where(far_l[:n], turn(ml[2, rows], -UNIT * g), x)
                fp[tile, t + 1, rows] = masked(x, r, n)
            return carry

        lax.fori_loop(0, CZ, rows_in, 0)
        lax.fori_loop(0, 4, columns_in, 0)

        def again(k, carry):
            def layer(i, carry):
                l = jnp.where(i < 2, i, i + 11)
                t, s = l // PER, lax.rem(l, PER)
                for r in (LO, OFF + BR):
                    p = turn(fp[k, t + 1, r : r + step], -(SLOT * s + HALF))
                    fa[k + 1, l + 1, r : r + step] = image_a(p, k, l + 1, r, step)[1]
                return carry

            def tile(i, carry):
                t = top_tile * i
                for r, n in segments(LO, HI):
                    own = [fa[k, PER * t + s + 1, r : r + n] for s in range(PER)]
                    fp[k + 1, t + 1, r : r + n] = image_p(own, k, t, r, n)
                return carry

            lax.fori_loop(0, 5, layer, 0)
            lax.fori_loop(0, 2, tile, 0)
            return carry

        lax.fori_loop(LOAD, LOAD + 3, again, 0)

    def make_tables():
        def mask(k, carry):
            fa[PAIRS, k, NLO:OFF] = fa[PAIRS, k, NLO:OFF] * top_ok
            fa[PAIRS, k, OFF + BR : NHI] = fa[PAIRS, k, OFF + BR : NHI] * bot_ok
            return carry

        lax.fori_loop(4, 8, mask, 0)

        def beside(u, carry):
            for r, n in segments(NLO, NHI):
                rows = slice(r, r + n)
                ok = row_ok_of(r)
                ok = lane_ok[:n] if ok is None else lane_ok[:n] * ok
                x = jnp.where(lane16[:n] >= BC - UNIT, turn(ml[3, rows], BC - UNIT - UNIT * u), 0.0)
                x = jnp.where(lane16[:n] < UNIT, turn(mr[3, rows], -UNIT * u), x)
                cb[u, rows] = jnp.where(u < 4, x, x * ok)
            return carry

        lax.fori_loop(0, 8, beside, 0)

        def table(c, carry):
            code_at = c.astype(F32)
            for r, n in inner:
                rows = slice(r, r + n)
                x = y = jnp.zeros((n, BC), F32)
                for k in range(4):
                    x = x + jnp.where(fa[PAIRS, k, rows] == code_at, fa[PAIRS, 4 + k, rows], 0.0)
                    y = y + jnp.where(cb[k, rows] == code_at, cb[4 + k, rows], 0.0)
                ta[c, rows] = x
                tb[c, rows] = y
            return carry

        lax.fori_loop(0, SPAN * SPAN, table, 0)

    def update(n, carry):
        k0 = LOAD + 4 * n
        zz = jnp.zeros((8, BC), F32)

        def power(j, carry):
            k = k0 + j

            def tile(t, sums):
                acc0, acc1 = sums
                for r, cnt in segments(NLO, NHI):
                    p = fp[k, t + 1, r : r + cnt]
                    own = []
                    for s in range(PER):
                        l = PER * t + s + 1
                        a, out = image_a(turn(p, -(SLOT * s + HALF)), k, l, r, cnt)
                        own.append(a)
                        if row_ok_of(r) is None:
                            acc0 = acc0 + fold(a * a)
                            acc1 = acc1 + fold(a * out)
                        fa[k + 1, l, r : r + cnt] = out
                    fp[k + 1, t + 1, r : r + cnt] = image_p(own, k, t, r, cnt)
                return acc0, acc1

            acc0, acc1 = lax.fori_loop(0, TILES, tile, (zz, zz))
            acc[2 * j] = acc0
            acc[2 * j + 1] = acc1
            return carry

        lax.fori_loop(0, 3, power, 0)

        row = jnp.zeros((1, BC), F32)
        for k in range(6):
            row = row + jnp.where(row_lane == k, jnp.sum(acc[k], keepdims=True), 0.0)
        mrow[n, 0] = row
        mbuf[n, me] = row

        def go(i, carry):
            pltpu.make_async_remote_copy(
                mrow.at[n, 0], mbuf.at[n, me], as_.at[n], ar.at[n], device_id=peer(i), device_id_type=MESH
            ).start()
            return carry

        lax.fori_loop(0, NPEER - 1, go, 0)

        send_early(n)
        when(n == 0)(far_tier)
        send_rest(n)
        when(n == 0)(make_tables)

        pltpu.make_async_copy(others(n), others(n), ar.at[n]).wait()
        total = jnp.sum(mbuf[n], axis=0)
        mz[n, 2] = total
        for c in relays(n):
            c.start()
        coefficients(total, n)

        @when(n == 0)
        def _():
            def residual(t, carry):
                c = [co[0, k] for k in range(3)]
                g = [1.0 - SHIFT * c[0], -(c[0] + SHIFT * c[1]), -(c[1] + SHIFT * c[2]), -c[2]]
                for r, cnt in inner:
                    rows = slice(r, r + cnt)
                    for ref, l in [(fp, t + 1)] + [(fa, PER * t + s + 1) for s in range(PER)]:
                        x = [g[k][:cnt] * ref[LOAD + k, l, rows] for k in range(4)]
                        ref[LOAD + 4, l, rows] = (x[0] + x[1]) + (x[2] + x[3])
                return carry

            lax.fori_loop(0, TILES, residual, 0)

        @when(n == 1)
        def _():
            def answer(l, carry):
                for r, cnt in chunks(OFF, OFF + BR, step):
                    x = combine(fa, LOAD, 0, l, r, cnt) + combine(fa, LOAD + 4, 1, l, r, cnt)
                    sol[l - 1, r - OFF : r - OFF + cnt] = x
                return carry

            lax.fori_loop(1, CZ + 1, answer, 0)

        for r, cnt in chunks(LO, HI, step):
            face[0, r : r + cnt] = combine(fa, k0, n, CZ, r, cnt)
            side_face[0, r : r + cnt] = turn(combine(fp, k0, n, TILES, r, cnt), HALF)

        for (r, cnt), x, y in zip(inner, *pull(0)):
            face[0, r : r + cnt] = x
            side_face[0, r : r + cnt] = y

        for c in relays(n) + faces(n, range(5)):
            c.wait()

        def solve(side, carry):
            coefficients(mz[n, side], 2 + side)
            return carry

        lax.fori_loop(0, 2, solve, 0)

        def from_body(side, where, r, cnt):
            at = slice(r - NLO, r - NLO + cnt)
            c = [co[where, k][:cnt] for k in range(3)]
            x = [c[k] * got[n, side, k, at] for k in range(3)]
            packed = got[n, side, 3, at]
            y = [c[k] * turn(packed, -(SLOT * k + HALF)) for k in range(3)]
            return (x[0] + x[1]) + x[2], (y[0] + y[1]) + y[2]

        for r in (LO, NHI):
            face[1, r : r + 8] = z8
            side_face[1, r : r + 8] = z8
        for r, cnt in inner:
            rows = slice(r, r + cnt)
            face[1, rows], side_face[1, rows] = from_body(1, 2, r, cnt)

        for (r, cnt), x, y in zip(inner, *pull(1)):
            face[1, r : r + cnt] = x
            side_face[1, r : r + cnt] = y

        for r, cnt in inner:
            rows = slice(r, r + cnt)
            x, y = from_body(0, 3, r, cnt)
            mult[0, rows] = 2.0 * mult[0, rows] + scale_up * (x - face[0, rows])
            mult[1, rows] = 2.0 * mult[1, rows] + scale_up * (y - side_face[0, rows])
            x = scale_dn * (combine(fa, k0, n, 1, r, cnt) - face[1, rows])
            low[rows] = 2.0 * low[rows] + x
        xs, ys = push()
        for (r, cnt), x, y in zip(inner, xs, ys):
            force[0, r : r + cnt] = x
            force[1, r : r + cnt] = y

        @when(n == 0)
        def _():
            for r, cnt in segments(NLO, NHI):
                rows = slice(r, r + cnt)
                ok = row_ok_of(r)
                x, y = force[0, rows], force[1, rows] * lane_ok[:cnt]
                if ok is not None:
                    x, y = x * ok, y * ok
                fa[LOAD + 4, CZ, rows] = fa[LOAD + 4, CZ, rows] + x
                back = jnp.where(high_slot[:cnt], turn(y, -HALF), 0.0)
                fp[LOAD + 4, TILES, rows] = fp[LOAD + 4, TILES, rows] + back
                fa[LOAD + 4, 1, rows] = fa[LOAD + 4, 1, rows] - low[rows]
                y = scale_dn * (turn(combine(fp, LOAD, 0, 1, r, cnt), -HALF) - side_face[1, rows])
                back = jnp.where(low_slot[:cnt], turn(y, HALF), 0.0)
                fp[LOAD + 4, 1, rows] = fp[LOAD + 4, 1, rows] - back

        return carry

    update(0, 0)
    update(1, 0)

    for r, n in chunks(OFF, OFF + BR, step):
        ifl[CZ - 1, r - OFF : r - OFF + n] = force[0, r : r + n]
        ifl[0, r - OFF : r - OFF + n] = -low[r : r + n]
    for c in near + late:
        c.wait_send()
    for n in range(2):
        pltpu.make_async_copy(others(n), others(n), as_.at[n]).wait()


def per_device(load, stiffness, pair_code, pair_weight):
    def plane(*lead):
        return pltpu.VMEM((*lead, ROWS, BC), F32)

    def vmem(*shape):
        return pltpu.VMEM((*shape, BC), F32)

    dma = pltpu.SemaphoreType.DMA
    nsend, near = 22, NHI - NLO
    scratch = [
        plane(10, CZ + 2), plane(10, TILES + 2), pltpu.VMEM((4, BR, BC), jnp.int32), plane(8),
        vmem(4, BR), vmem(4, BR), plane(4), plane(4), vmem(2, 2, CZ, 8),
        plane(SPAN * SPAN), plane(SPAN * SPAN), plane(), plane(), plane(2), plane(2), plane(2), plane(), plane(2),
        vmem(2, 4, near), vmem(2, near), vmem(2, 2, 4, near), vmem(6, 8), vmem(4, 3, 16),
        vmem(2, 1, 1), vmem(2, NPEER, 1), vmem(2, 3, 1),
        dma((4,)), dma((nsend,)), dma((nsend,)), dma((2, 5)), dma((2, 5)),
        dma((2,)), dma((2,)), dma((2, 2)), dma((2, 2)),
    ]
    return pl.pallas_call(
        kernel,
        out_shape=(pltpu.VMEM((CZ, BR, BC), F32),) * 2,
        in_specs=[pl.BlockSpec(memory_space=pl.ANY)] * 4,
        out_specs=[pl.BlockSpec(memory_space=pltpu.VMEM)] * 2,
        scratch_shapes=scratch,
        compiler_params=pltpu.CompilerParams(collective_id=0, has_side_effects=True),
        name="uzawa",
    )(load, stiffness, pair_code, pair_weight)


def solution(mesh):
    return jax.shard_map(
        per_device,
        mesh=mesh,
        in_specs=(
            P("body", "gx", "gy"),
            P("body", "gx", "gy"),
            P(None, "gx", "gy"),
            P(None, "gx", "gy"),
        ),
        out_specs=(P("body", "gx", "gy"), P("body", "gx", "gy")),
        check_vma=False,
    )
```

```python
import jax
import jax.numpy as jnp
from jax import lax
from jax.experimental import pallas as pl
from jax.experimental.pallas import tpu as pltpu
from jax.sharding import PartitionSpec as P

MESH = pl.DeviceIdType.MESH
F32 = jnp.float32

NBODY, NGX, NGY = 8, 8, 4
NPEER = NGX * NGY
CZ, BR, BC = 16, 64, 128
REACH, SPAN, RATE = 2, 5, 2.0
OFF = 24
ROWS = BR + 2 * OFF
LO, HI = 8, ROWS - 8
NLO, NHI = 16, ROWS - 16
SLOT, HALF = 32, 16
PER = BC // SLOT
TILES = CZ // PER
UNIT = 8
SHIFT = 6.0
STIFF, LOAD, PAIRS = 0, 1, 9


def turn(x, by):
    if isinstance(by, int):
        by %= BC
        return x if by == 0 else pltpu.roll(x, by, x.ndim - 1)
    return pltpu.roll(x, lax.rem(by + BC, BC), x.ndim - 1)


def when(flag):
    return lambda f: f() if flag else None


def chunks(first, last, step):
    return [(r, min(step, last - r)) for r in range(first, last, step)]


def kernel(
    load, stiff, code, weight, sol, ifl,
    fa, fp, ci, cb, sl, sr, ml, mr, far, ta, tb, sha, shb, face, side_face, mult, low, force,
    stage, stage_low, got, acc, co, mrow, mbuf, mz,
    lsem, rs, rr, fs, fr, as_, ar, zs, zr,
):
    body, gx, gy = (lax.axis_index(n) for n in ("body", "gx", "gy"))
    me = gx * NGY + gy
    gxm, gxp = lax.rem(gx + NGX - 1, NGX), lax.rem(gx + 1, NGX)
    gym, gyp = lax.rem(gy + NGY - 1, NGY), lax.rem(gy + 1, NGY)
    below, above = lax.rem(body + NBODY - 1, NBODY), lax.rem(body + 1, NBODY)

    def peer(i):
        o = i + 12
        o = jnp.where(o >= NPEER, o - (NPEER - 1), o)
        p = me + o
        p = jnp.where(p >= NPEER, p - NPEER, p)
        return (body, lax.div(p, NGY), lax.rem(p, NGY))

    barrier = pltpu.get_barrier_semaphore()

    def greet(i, carry):
        pl.semaphore_signal(barrier, inc=1, device_id=peer(i), device_id_type=MESH)
        return carry

    lax.fori_loop(0, NPEER - 1, greet, 0)
    pl.semaphore_signal(barrier, inc=1, device_id=(below, gx, gy), device_id_type=MESH)
    pl.semaphore_signal(barrier, inc=1, device_id=(above, gx, gy), device_id_type=MESH)

    own_rows = pl.ds(OFF, BR)
    locals_ = [
        pltpu.make_async_copy(stiff, fa.at[STIFF, pl.ds(1, CZ), own_rows, :], lsem.at[0]),
        pltpu.make_async_copy(load, fa.at[LOAD, pl.ds(1, CZ), own_rows, :], lsem.at[1]),
        pltpu.make_async_copy(code, ci, lsem.at[2]),
        pltpu.make_async_copy(weight, fa.at[PAIRS, pl.ds(4, 4), own_rows, :], lsem.at[3]),
    ]
    for c in locals_:
        c.start()

    one = jnp.float32(1.0)
    zero = jnp.float32(0.0)
    top_ok = jnp.where(gx > 0, one, zero)
    bot_ok = jnp.where(gx < NGX - 1, one, zero)
    right_ok = jnp.where(gy < NGY - 1, one, zero)
    left_ok = jnp.where(gy > 0, one, zero)
    scale_up = jnp.where(body < NBODY - 1, jnp.float32(RATE), zero)
    scale_dn = jnp.where(body > 0, jnp.float32(RATE), zero)

    step = 16
    z16 = jnp.zeros((step, BC), F32)
    z8 = jnp.zeros((8, BC), F32)

    def zero_ends(i, carry):
        for r, n in chunks(0, ROWS, step):
            for l in (0, CZ + 1):
                fa[i + LOAD, l, r : r + n] = z16
            for t in (0, TILES + 1):
                fp[i + LOAD, t, r : r + n] = z16
        return carry

    def zero_far(l, carry):
        for r in (LO, NHI):
            for k in range(4):
                fa[k, l, r : r + 8] = z8
        return carry

    lax.fori_loop(0, 8, zero_ends, 0)
    lax.fori_loop(1, CZ + 1, zero_far, 0)
    for k in range(2):
        for r in (LO, NHI):
            mult[k, r : r + 8] = z8
            for t in range(TILES):
                fp[k, t + 1, r : r + 8] = z8
        for r, n in chunks(NLO, NHI, step):
            mult[k, r : r + n] = z16
    for r, n in chunks(NLO, NHI, step):
        low[r : r + n] = z16

    lane8 = lax.broadcasted_iota(jnp.int32, (8, BC), 1)
    top_tile = TILES - 1
    units = [(u // PER, u % PER) for u in range(16)]

    def put(tile, i, items, skip):
        left = right = None
        for u, (field, layer) in enumerate(items):
            x = fa[field, layer, pl.ds(pl.multiple_of(8 * i + OFF, 8), 8), :]
            x_l, x_r = turn(x, UNIT * u - skip), turn(x, UNIT * u + UNIT + skip)
            left = x_l if u == 0 else jnp.where(lane8 >= UNIT * u, x_l, left)
            right = x_r if u == 0 else jnp.where(lane8 >= UNIT * u, x_r, right)
        at = pl.ds(pl.multiple_of(8 * i, 8), 8)
        sl[tile, at, :] = left
        sr[tile, at, :] = right

    def pack_near(i, carry):
        for tile in (STIFF, LOAD):
            put(tile, i, [(tile, 1 + PER * t + s) for s, t in units], 0)
        return carry

    def pack_far(i, carry):
        put(2, i, [(t // 2, 1 + PER * top_tile * (t % 2) + s) for s, t in units], UNIT)
        put(3, i, [(PAIRS, k) for k in range(8)], 0)
        return carry

    for c in locals_:
        c.wait()
    lax.fori_loop(0, BR // 8, pack_near, 0)
    pl.semaphore_wait(barrier, NPEER - 1 + 2)

    count = [0]

    def send(src, dst, dev):
        n = count[0]
        count[0] += 1
        c = pltpu.make_async_remote_copy(src, dst, rs.at[n], rr.at[n], device_id=dev, device_id_type=MESH)
        c.start()
        return c

    near = []
    two = pl.ds(0, 2)
    ways = ((sl, mr, gym), (sr, ml, gyp))
    for buf, dst, dev_y in ways:
        near.append(send(buf.at[two], dst.at[two, own_rows, :], (body, gx, dev_y)))
    sides = (
        ((body, gxm, gy), OFF, OFF + BR, OFF + 8),
        ((body, gxp, gy), OFF + BR - 8, NLO, OFF + BR - 16),
    )
    layers = pl.ds(1, CZ)
    for dev, row, to, _ in sides:
        near.append(send(fa.at[two, layers, pl.ds(row, 8), :], fa.at[two, layers, pl.ds(to, 8), :], dev))
    for buf, dst, dev_y in ways:
        near.append(send(buf.at[two, pl.ds(0, 8), :], dst.at[two, pl.ds(OFF + BR, 8), :], (body, gxm, dev_y)))
        near.append(send(buf.at[two, pl.ds(BR - 8, 8), :], dst.at[two, pl.ds(NLO, 8), :], (body, gxp, dev_y)))

    for k in range(4):
        fa[PAIRS, k, OFF : OFF + BR] = ci[k].astype(F32)
    lax.fori_loop(0, BR // 8, pack_far, 0)
    late = []
    rest = pl.ds(2, 2)
    for buf, dst, dev_y in ways:
        late.append(send(buf.at[rest], dst.at[rest, own_rows, :], (body, gx, dev_y)))
        late.append(send(buf.at[rest, pl.ds(0, 16), :], dst.at[rest, pl.ds(OFF + BR, 16), :], (body, gxm, dev_y)))
        late.append(send(buf.at[rest, pl.ds(BR - 16, 16), :], dst.at[rest, pl.ds(LO, 16), :], (body, gxp, dev_y)))
        late.append(send(buf.at[two, pl.ds(8, 8), :], dst.at[two, pl.ds(NHI, 8), :], (body, gxm, dev_y)))
        late.append(send(buf.at[two, pl.ds(BR - 16, 8), :], dst.at[two, pl.ds(LO, 8), :], (body, gxp, dev_y)))
    pairs = pl.ds(0, 8)
    for side, (dev, row, to, far_row) in enumerate(sides):
        late.append(send(fa.at[two, layers, pl.ds(far_row, 8), :], far.at[side], dev))
        late.append(send(fa.at[PAIRS, pairs, pl.ds(row, 8), :], fa.at[PAIRS, pairs, pl.ds(to, 8), :], dev))

    def clear(l, carry):
        for r, n in chunks(0, BR, step):
            ifl[l, r : r + n] = z16
        return carry

    lax.fori_loop(1, CZ - 1, clear, 0)

    def entry(x_ref, lead, c, r, n):
        rows = slice(r, r + n)
        x = jnp.zeros((n, BC), F32)
        for k in range(4):
            x = x + jnp.where(x_ref[lead + (k, rows)] == c.astype(F32), x_ref[lead + (4 + k, rows)], 0.0)
        return x

    def own_table(c, carry):
        for r, n in chunks(OFF, OFF + BR, step):
            ta[c, r : r + n] = entry(fa, (PAIRS,), c, r, n)
        return carry

    lane16 = lax.broadcasted_iota(jnp.int32, (step, BC), 1)
    first, last = lane16 == 0, lane16 == BC - 1
    lane_ok = jnp.where(lane16 < BC // 2, right_ok, left_ok)
    in_slot = lax.bitwise_and(lane16, SLOT - 1)
    slot_ok = jnp.where(in_slot < HALF, left_ok, right_ok)
    is_l0, is_r0 = in_slot == HALF - 1, in_slot == HALF
    near_l = (in_slot >= UNIT) & (in_slot < HALF)
    near_r = (in_slot >= HALF) & (in_slot < HALF + UNIT)
    far_l, far_r = in_slot < UNIT, in_slot >= SLOT - UNIT
    low_slot, high_slot = lane16 < SLOT, lane16 >= BC - SLOT

    def row_ok_of(r):
        return top_ok if r < OFF else bot_ok if r >= OFF + BR else None

    def segments(lo, hi):
        return chunks(lo, OFF, step) + chunks(OFF, OFF + BR, step) + chunks(OFF + BR, hi, step)

    def fold(x):
        return jnp.sum(x.reshape(x.shape[0] // 8, 8, BC), axis=0)

    def masked(x, r, n):
        ok = row_ok_of(r)
        x = x * slot_ok[:n]
        return x if ok is None else x * ok

    def columns(tile, t, r, n):
        rows = slice(r, r + n)
        x = jnp.where(near_r[:n], turn(mr[tile, rows], HALF - UNIT * t), 0.0)
        return jnp.where(near_l[:n], turn(ml[tile, rows], UNIT - UNIT * t), x)

    lax.fori_loop(0, SPAN * SPAN, own_table, 0)
    for c in near:
        c.wait_recv()

    def unpack(i, carry):
        tile, t = i // TILES, lax.rem(i, TILES)
        for r, n in segments(NLO, NHI):
            fp[tile, t + 1, r : r + n] = masked(columns(tile, t, r, n), r, n)
        return carry

    def mask_rows(l, carry):
        fa[LOAD, l, NLO:OFF] = fa[LOAD, l, NLO:OFF] * top_ok
        fa[LOAD, l, OFF + BR : NHI] = fa[LOAD, l, OFF + BR : NHI] * bot_ok
        return carry

    lax.fori_loop(0, 2 * TILES, unpack, 0)
    lax.fori_loop(1, CZ + 1, mask_rows, 0)

    def image_a(p, k, l, r, n):
        rows = slice(r, r + n)
        a = fa[k, l, rows]
        s = turn(jnp.where(last[:n], p, a), 1) + turn(jnp.where(first[:n], p, a), -1)
        s = s + (fa[k, l, r - 1 : r - 1 + n] + fa[k, l, r + 1 : r + 1 + n])
        s = s + (fa[k, l - 1, rows] + fa[k, l + 1, rows])
        out = fa[STIFF, l, rows] * a - s
        ok = row_ok_of(r)
        return a, out if ok is None else out * ok

    def image_p(own, k, t, r, n):
        edge = None
        for s in range(PER):
            x = turn(own[s], SLOT * s + HALF)
            edge = x if s == 0 else jnp.where(lane16[:n] >= SLOT * s, x, edge)
        rows = slice(r, r + n)
        p = fp[k, t + 1, rows]
        s = turn(jnp.where(is_l0[:n], edge, p), 1) + turn(jnp.where(is_r0[:n], edge, p), -1)
        s = s + (fp[k, t + 1, r - 1 : r - 1 + n] + fp[k, t + 1, r + 1 : r + 1 + n])
        s = s + turn(jnp.where(high_slot[:n], fp[k, t, rows], p), SLOT)
        s = s + turn(jnp.where(low_slot[:n], fp[k, t + 2, rows], p), -SLOT)
        return masked(fp[STIFF, t + 1, rows] * p - s, r, n)

    row_lane = lax.broadcasted_iota(jnp.int32, (1, BC), 1)

    def others(n):
        return mbuf.at[n, pl.ds(0, NPEER - 1)]

    def relays(n):
        return [
            pltpu.make_async_remote_copy(
                mz.at[n, 2], mz.at[n, side], zs.at[n, side], zr.at[n, side],
                device_id=(dev, gx, gy), device_id_type=MESH,
            )
            for side, dev in ((0, above), (1, below))
        ]

    def faces(n, which):
        k0 = pl.ds(LOAD + 4 * n, 3)

        def part(to, size):
            return fa.at[k0, 1, pl.ds(NLO + to, size), :], got.at[n, 0, pl.ds(0, 3), pl.ds(to, size), :]

        far_part = NHI - NLO - 8
        pairs_ = (
            (stage.at[n], got.at[n, 1], above),
            (*part(8, BR), below),
            (*part(0, 8), below),
            (*part(far_part, 8), below),
            (stage_low.at[n], got.at[n, 0, 3], below),
        )
        return [
            pltpu.make_async_remote_copy(
                x, y, fs.at[n, i], fr.at[n, i], device_id=(dev, gx, gy), device_id_type=MESH
            )
            for i, (x, y, dev) in enumerate(pairs_)
            if i in which
        ]

    def side_columns(k0, t, slot, r, cnt):
        x = None
        for k in range(3):
            y = turn(fp[k0 + k, t, r : r + cnt], SLOT * (k - slot))
            x = y if k == 0 else jnp.where(lane16[:cnt] >= SLOT * k, y, x)
        return x

    def send_early(n):
        k0 = LOAD + 4 * n
        for r, cnt in chunks(NLO, NHI, step):
            at = slice(r - NLO, r - NLO + cnt)
            for k in range(3):
                stage[n, k, at] = fa[k0 + k, CZ, r : r + cnt]
            stage[n, 3, at] = side_columns(k0, TILES, PER - 1, r, cnt)
        for c in faces(n, (0, 1)):
            c.start()

    def send_rest(n):
        k0 = LOAD + 4 * n
        for r, cnt in chunks(NLO, NHI, step):
            stage_low[n, r - NLO : r - NLO + cnt] = side_columns(k0, 1, 0, r, cnt)
        for c in faces(n, (2, 3, 4)):
            c.start()

    def coefficients(total, where):
        m = [jnp.sum(jnp.where(row_lane == k, total, 0.0), axis=1, keepdims=True) for k in range(6)]
        h = [m[k + 1] + SHIFT * m[k] for k in range(5)]
        inv = 1.0 / h[0]
        l10, l20 = h[1] * inv, h[2] * inv
        d1 = h[2] - l10 * h[1]
        e12 = h[3] - l20 * h[1]
        inv1 = 1.0 / d1
        l21 = e12 * inv1
        d2 = h[4] - l20 * h[2] - l21 * e12
        y1 = m[1] - l10 * m[0]
        y2 = m[2] - l20 * m[0] - l21 * y1
        c2 = y2 / d2
        c1 = y1 * inv1 - l21 * c2
        c0 = m[0] * inv - l10 * c1 - l20 * c2
        for k, c in enumerate((c0, c1, c2)):
            co[where, k] = jnp.broadcast_to(c, (step, BC))

    def combine(ref, k0, where, l, r, n):
        rows = slice(r, r + n)
        x = [co[where, k][:n] * ref[k0 + k, l, rows] for k in range(3)]
        return (x[0] + x[1]) + x[2]

    def moved(a, b, by):
        at = lane16[: a.shape[0]] - by
        late_ = (at < 0) | (at > BC - 1)
        return turn(jnp.where(late_, b, a), -by), turn(jnp.where(late_, a, b), -by)

    inner = chunks(NLO, NHI, step)
    block = chunks(OFF, OFF + BR, step)

    def nothing(pieces):
        return tuple(jnp.zeros((n, BC), F32) for _, n in pieces)

    def pull(side, pieces=inner, beside=True):
        def one(d, sums):
            xs, ys = sums
            for r, n in chunks(LO, HI, step):
                rows = slice(r, r + n)
                sha[rows], shb[rows] = moved(face[side, rows], side_face[side, rows], d - REACH)
            out_x, out_y = [], []
            for (r, n), x, y in zip(pieces, xs, ys):
                for dx in range(SPAN):
                    c, q = dx * SPAN + d, r + dx - REACH
                    x = x + ta[c, r : r + n] * sha[q : q + n]
                    if beside:
                        y = y + tb[c, r : r + n] * shb[q : q + n]
                out_x.append(x)
                out_y.append(y)
            return tuple(out_x), tuple(out_y)

        return lax.fori_loop(0, SPAN, one, (nothing(pieces), nothing(pieces)))

    def push(pieces):
        def one(d, sums):
            xs, ys = sums
            out_x, out_y = [], []
            for (r, n), x, y in zip(pieces, xs, ys):
                p = q = jnp.zeros((n, BC), F32)
                for dx in range(SPAN):
                    c, o = dx * SPAN + d, r - dx + REACH
                    p = p + ta[c, o : o + n] * mult[0, o : o + n]
                    q = q + tb[c, o : o + n] * mult[1, o : o + n]
                p, q = moved(p, q, REACH - d)
                out_x.append(x + p)
                out_y.append(y + q)
            return tuple(out_x), tuple(out_y)

        return lax.fori_loop(0, SPAN, one, (nothing(pieces), nothing(pieces)))

    def far_tier():
        for c in late:
            c.wait_recv()

        def rows_in(l, carry):
            for side, (r, ok) in enumerate(((NHI, bot_ok), (LO, top_ok))):
                for k in range(2):
                    fa[k, l + 1, r : r + 8] = far[side, k, l] * ok
            return carry

        def columns_in(i, carry):
            tile, f = i // 2, lax.rem(i, 2)
            g = f + 2 * tile
            t = top_tile * f
            for r, n in segments(LO, HI):
                rows = slice(r, r + n)
                x = jnp.where(far_r[:n], turn(mr[2, rows], SLOT - UNIT - UNIT * g), columns(tile, t, r, n))
                x = jnp.where(far_l[:n], turn(ml[2, rows], -UNIT * g), x)
                fp[tile, t + 1, rows] = masked(x, r, n)
            return carry

        lax.fori_loop(0, CZ, rows_in, 0)
        lax.fori_loop(0, 4, columns_in, 0)

        def again(k, carry):
            def layer(i, carry):
                l = jnp.where(i < 2, i, i + 11)
                t, s = l // PER, lax.rem(l, PER)
                for r in (LO, OFF + BR):
                    p = turn(fp[k, t + 1, r : r + step], -(SLOT * s + HALF))
                    fa[k + 1, l + 1, r : r + step] = image_a(p, k, l + 1, r, step)[1]
                return carry

            def tile(i, carry):
                t = top_tile * i
                for r, n in segments(LO, HI):
                    own = [fa[k, PER * t + s + 1, r : r + n] for s in range(PER)]
                    fp[k + 1, t + 1, r : r + n] = image_p(own, k, t, r, n)
                return carry

            lax.fori_loop(0, 5, layer, 0)
            lax.fori_loop(0, 2, tile, 0)
            return carry

        lax.fori_loop(LOAD, LOAD + 3, again, 0)

    def side_pairs():
        def mask(k, carry):
            fa[PAIRS, k, NLO:OFF] = fa[PAIRS, k, NLO:OFF] * top_ok
            fa[PAIRS, k, OFF + BR : NHI] = fa[PAIRS, k, OFF + BR : NHI] * bot_ok
            return carry

        lax.fori_loop(4, 8, mask, 0)

        def beside(u, carry):
            for r, n in segments(NLO, NHI):
                rows = slice(r, r + n)
                ok = row_ok_of(r)
                ok = lane_ok[:n] if ok is None else lane_ok[:n] * ok
                x = jnp.where(lane16[:n] >= BC - UNIT, turn(ml[3, rows], BC - UNIT - UNIT * u), 0.0)
                x = jnp.where(lane16[:n] < UNIT, turn(mr[3, rows], -UNIT * u), x)
                cb[u, rows] = jnp.where(u < 4, x, x * ok)
            return carry

        lax.fori_loop(0, 8, beside, 0)

    def outer_table(c, carry):
        for r in (NLO, OFF + BR):
            ta[c, r : r + 8] = entry(fa, (PAIRS,), c, r, 8)
        for r, n in inner:
            tb[c, r : r + n] = entry(cb, (), c, r, n)
        return carry


    def zero_sums():
        for k in range(6):
            acc[k] = z8

    def powers(k0, count, which, keep=True):
        def one(i, carry):
            j, t = which(i)
            k = k0 + j
            acc0 = acc1 = jnp.zeros((8, BC), F32)
            for r, cnt in segments(NLO, NHI) if keep else chunks(OFF, OFF + BR, step):
                p = fp[k, t + 1, r : r + cnt]
                own = []
                for s in range(PER):
                    l = PER * t + s + 1
                    a, out = image_a(turn(p, -(SLOT * s + HALF)), k, l, r, cnt)
                    own.append(a)
                    if row_ok_of(r) is None:
                        acc0 = acc0 + fold(a * a)
                        acc1 = acc1 + fold(a * out)
                    if keep:
                        fa[k + 1, l, r : r + cnt] = out
                if keep:
                    fp[k + 1, t + 1, r : r + cnt] = image_p(own, k, t, r, cnt)
            acc[2 * j] = acc[2 * j] + acc0
            acc[2 * j + 1] = acc[2 * j + 1] + acc1
            return carry

        lax.fori_loop(0, count, one, 0)

    def update(n, carry):
        k0 = LOAD + 4 * n
        if n == 0:
            zero_sums()
            powers(k0, 3 * TILES, lambda i: (lax.div(i, TILES), lax.rem(i, TILES)))
        else:
            powers(
                k0,
                2 + TILES,
                lambda i: (jnp.where(i < 2, 0, 1), jnp.where(i < 2, top_tile * i, i - 2)),
            )
            powers(k0, TILES, lambda i: (2, i), keep=False)

        row = jnp.zeros((1, BC), F32)
        for k in range(6):
            row = row + jnp.where(row_lane == k, jnp.sum(acc[k], keepdims=True), 0.0)
        mrow[n, 0] = row
        mbuf[n, me] = row

        def go(i, carry):
            pltpu.make_async_remote_copy(
                mrow.at[n, 0], mbuf.at[n, me], as_.at[n], ar.at[n], device_id=peer(i), device_id_type=MESH
            ).start()
            return carry

        lax.fori_loop(0, NPEER - 1, go, 0)

        send_early(n)
        when(n == 0)(far_tier)
        send_rest(n)
        when(n == 0)(side_pairs)

        pltpu.make_async_copy(others(n), others(n), ar.at[n]).wait()
        total = jnp.sum(mbuf[n], axis=0)
        mz[n, 2] = total
        for c in relays(n):
            c.start()
        coefficients(total, n)

        @when(n == 0)
        def _():
            def residual(t, carry):
                c = [co[0, k] for k in range(3)]
                g = [1.0 - SHIFT * c[0], -(c[0] + SHIFT * c[1]), -(c[1] + SHIFT * c[2]), -c[2]]
                for r, cnt in inner:
                    rows = slice(r, r + cnt)
                    for ref, l in [(fp, t + 1)] + [(fa, PER * t + s + 1) for s in range(PER)]:
                        x = [g[k][:cnt] * ref[LOAD + k, l, rows] for k in range(4)]
                        ref[LOAD + 4, l, rows] = (x[0] + x[1]) + (x[2] + x[3])
                return carry

            lax.fori_loop(0, TILES, residual, 0)
            lax.fori_loop(0, SPAN * SPAN, outer_table, 0)

        @when(n == 1)
        def _():
            def answer(l, carry):
                for r, cnt in chunks(OFF, OFF + BR, step):
                    x = combine(fa, LOAD, 0, l, r, cnt) + combine(fa, LOAD + 4, 1, l, r, cnt)
                    sol[l - 1, r - OFF : r - OFF + cnt] = x
                return carry

            lax.fori_loop(1, CZ + 1, answer, 0)

        for r, cnt in chunks(LO, HI, step):
            face[0, r : r + cnt] = combine(fa, k0, n, CZ, r, cnt)
            side_face[0, r : r + cnt] = turn(combine(fp, k0, n, TILES, r, cnt), HALF)

        for (r, cnt), x, y in zip(inner, *pull(0)):
            face[0, r : r + cnt] = x
            side_face[0, r : r + cnt] = y
        if n == 0:
            zero_sums()
            powers(LOAD + 4, TILES - 2, lambda i: (0, i + 1))

        for c in relays(n) + faces(n, range(5)):
            c.wait()

        def solve(side, carry):
            coefficients(mz[n, side], 2 + side)
            return carry

        lax.fori_loop(0, 2, solve, 0)

        def from_body(side, where, r, cnt):
            at = slice(r - NLO, r - NLO + cnt)
            c = [co[where, k][:cnt] for k in range(3)]
            x = [c[k] * got[n, side, k, at] for k in range(3)]
            packed = got[n, side, 3, at]
            y = [c[k] * turn(packed, -(SLOT * k + HALF)) for k in range(3)]
            return (x[0] + x[1]) + x[2], (y[0] + y[1]) + y[2]

        for r in (LO, NHI):
            face[1, r : r + 8] = z8
            side_face[1, r : r + 8] = z8
        for r, cnt in inner:
            rows = slice(r, r + cnt)
            face[1, rows], side_face[1, rows] = from_body(1, 2, r, cnt)

        pieces = inner if n == 0 else block
        for (r, cnt), x, y in zip(pieces, *pull(1, pieces, n == 0)):
            face[1, r : r + cnt] = x
            side_face[1, r : r + cnt] = y

        for r, cnt in inner:
            rows = slice(r, r + cnt)
            x, y = from_body(0, 3, r, cnt)
            mult[0, rows] = 2.0 * mult[0, rows] + scale_up * (x - face[0, rows])
            mult[1, rows] = 2.0 * mult[1, rows] + scale_up * (y - side_face[0, rows])
            x = scale_dn * (combine(fa, k0, n, 1, r, cnt) - face[1, rows])
            low[rows] = 2.0 * low[rows] + x
        for (r, cnt), x, y in zip(pieces, *push(pieces)):
            force[0, r : r + cnt] = x
            if n == 0:
                force[1, r : r + cnt] = y

        @when(n == 0)
        def _():
            for r, cnt in segments(NLO, NHI):
                rows = slice(r, r + cnt)
                ok = row_ok_of(r)
                x, y = force[0, rows], force[1, rows] * lane_ok[:cnt]
                if ok is not None:
                    x, y = x * ok, y * ok
                fa[LOAD + 4, CZ, rows] = fa[LOAD + 4, CZ, rows] + x
                back = jnp.where(high_slot[:cnt], turn(y, -HALF), 0.0)
                fp[LOAD + 4, TILES, rows] = fp[LOAD + 4, TILES, rows] + back
                fa[LOAD + 4, 1, rows] = fa[LOAD + 4, 1, rows] - low[rows]
                y = scale_dn * (turn(combine(fp, LOAD, 0, 1, r, cnt), -HALF) - side_face[1, rows])
                back = jnp.where(low_slot[:cnt], turn(y, HALF), 0.0)
                fp[LOAD + 4, 1, rows] = fp[LOAD + 4, 1, rows] - back

        return carry

    update(0, 0)
    update(1, 0)

    for r, n in chunks(OFF, OFF + BR, step):
        ifl[CZ - 1, r - OFF : r - OFF + n] = force[0, r : r + n]
        ifl[0, r - OFF : r - OFF + n] = -low[r : r + n]
    for c in near + late:
        c.wait_send()
    for n in range(2):
        pltpu.make_async_copy(others(n), others(n), as_.at[n]).wait()


def per_device(load, stiffness, pair_code, pair_weight):
    def plane(*lead):
        return pltpu.VMEM((*lead, ROWS, BC), F32)

    def vmem(*shape):
        return pltpu.VMEM((*shape, BC), F32)

    dma = pltpu.SemaphoreType.DMA
    nsend, near = 22, NHI - NLO
    scratch = [
        plane(10, CZ + 2), plane(10, TILES + 2), pltpu.VMEM((4, BR, BC), jnp.int32), plane(8),
        vmem(4, BR), vmem(4, BR), plane(4), plane(4), vmem(2, 2, CZ, 8),
        plane(SPAN * SPAN), plane(SPAN * SPAN), plane(), plane(), plane(2), plane(2), plane(2), plane(), plane(2),
        vmem(2, 4, near), vmem(2, near), vmem(2, 2, 4, near), vmem(6, 8), vmem(4, 3, 16),
        vmem(2, 1, 1), vmem(2, NPEER, 1), vmem(2, 3, 1),
        dma((4,)), dma((nsend,)), dma((nsend,)), dma((2, 5)), dma((2, 5)),
        dma((2,)), dma((2,)), dma((2, 2)), dma((2, 2)),
    ]
    return pl.pallas_call(
        kernel,
        out_shape=(pltpu.VMEM((CZ, BR, BC), F32),) * 2,
        in_specs=[pl.BlockSpec(memory_space=pl.ANY)] * 4,
        out_specs=[pl.BlockSpec(memory_space=pltpu.VMEM)] * 2,
        scratch_shapes=scratch,
        compiler_params=pltpu.CompilerParams(collective_id=0, has_side_effects=True),
        name="uzawa",
    )(load, stiffness, pair_code, pair_weight)


def solution(mesh):
    return jax.shard_map(
        per_device,
        mesh=mesh,
        in_specs=(
            P("body", "gx", "gy"),
            P("body", "gx", "gy"),
            P(None, "gx", "gy"),
            P(None, "gx", "gy"),
        ),
        out_specs=(P("body", "gx", "gy"), P("body", "gx", "gy")),
        check_vma=False,
    )
```

```python
import jax
import jax.numpy as jnp
from jax import lax
from jax.experimental import pallas as pl
from jax.experimental.pallas import tpu as pltpu
from jax.sharding import PartitionSpec as P

MESH = pl.DeviceIdType.MESH
F32 = jnp.float32

NBODY, NGX, NGY = 8, 8, 4
NPEER = NGX * NGY
CZ, BR, BC = 16, 64, 128
REACH, SPAN, RATE = 2, 5, 2.0
OFF = 24
ROWS = BR + 2 * OFF
LO, HI = 8, ROWS - 8
NLO, NHI = 16, ROWS - 16
SLOT, HALF = 32, 16
PER = BC // SLOT
TILES = CZ // PER
UNIT = 8
SHIFT = 6.0
STIFF, LOAD, PAIRS = 0, 1, 9


def turn(x, by):
    if isinstance(by, int):
        by %= BC
        return x if by == 0 else pltpu.roll(x, by, x.ndim - 1)
    return pltpu.roll(x, lax.rem(by + BC, BC), x.ndim - 1)


def when(flag):
    return lambda f: f() if flag else None


def chunks(first, last, step):
    return [(r, min(step, last - r)) for r in range(first, last, step)]


def kernel(
    load, stiff, code, weight, sol, ifl,
    fa, fp, ci, cb, sl, sr, ml, mr, far, ta, tb, sha, shb, face, side_face, mult, low, force,
    stage, stage_low, got, acc, co, mrow, mbuf, mz,
    lsem, rs, rr, fs, fr, as_, ar, zs, zr,
):
    body, gx, gy = (lax.axis_index(n) for n in ("body", "gx", "gy"))
    me = gx * NGY + gy
    gxm, gxp = lax.rem(gx + NGX - 1, NGX), lax.rem(gx + 1, NGX)
    gym, gyp = lax.rem(gy + NGY - 1, NGY), lax.rem(gy + 1, NGY)
    below, above = lax.rem(body + NBODY - 1, NBODY), lax.rem(body + 1, NBODY)

    def peer(i):
        o = i + 12
        o = jnp.where(o >= NPEER, o - (NPEER - 1), o)
        p = me + o
        p = jnp.where(p >= NPEER, p - NPEER, p)
        return (body, lax.div(p, NGY), lax.rem(p, NGY))

    barrier = pltpu.get_barrier_semaphore()

    def greet(i, carry):
        pl.semaphore_signal(barrier, inc=1, device_id=peer(i), device_id_type=MESH)
        return carry

    own_rows = pl.ds(OFF, BR)
    locals_ = [
        pltpu.make_async_copy(stiff, fa.at[STIFF, pl.ds(1, CZ), own_rows, :], lsem.at[0]),
        pltpu.make_async_copy(load, fa.at[LOAD, pl.ds(1, CZ), own_rows, :], lsem.at[1]),
        pltpu.make_async_copy(code, ci, lsem.at[2]),
        pltpu.make_async_copy(weight, fa.at[PAIRS, pl.ds(4, 4), own_rows, :], lsem.at[3]),
    ]
    for c in locals_:
        c.start()
    lax.fori_loop(0, NPEER - 1, greet, 0)
    pl.semaphore_signal(barrier, inc=1, device_id=(below, gx, gy), device_id_type=MESH)
    pl.semaphore_signal(barrier, inc=1, device_id=(above, gx, gy), device_id_type=MESH)

    one = jnp.float32(1.0)
    zero = jnp.float32(0.0)
    top_ok = jnp.where(gx > 0, one, zero)
    bot_ok = jnp.where(gx < NGX - 1, one, zero)
    right_ok = jnp.where(gy < NGY - 1, one, zero)
    left_ok = jnp.where(gy > 0, one, zero)
    scale_up = jnp.where(body < NBODY - 1, jnp.float32(RATE), zero)
    scale_dn = jnp.where(body > 0, jnp.float32(RATE), zero)

    step = 16
    z16 = jnp.zeros((step, BC), F32)
    z8 = jnp.zeros((8, BC), F32)

    def zero_ends(i, carry):
        for r, n in chunks(0, ROWS, step):
            for l in (0, CZ + 1):
                fa[i + LOAD, l, r : r + n] = z16
            for t in (0, TILES + 1):
                fp[i + LOAD, t, r : r + n] = z16
        return carry

    def zero_far(l, carry):
        for r in (LO, NHI):
            for k in range(4):
                fa[k, l, r : r + 8] = z8
        return carry

    lax.fori_loop(0, 8, zero_ends, 0)
    lax.fori_loop(1, CZ + 1, zero_far, 0)
    for k in range(2):
        for r in (LO, NHI):
            mult[k, r : r + 8] = z8
            for t in range(TILES):
                fp[k, t + 1, r : r + 8] = z8
        for r, n in chunks(NLO, NHI, step):
            mult[k, r : r + n] = z16
    for r, n in chunks(NLO, NHI, step):
        low[r : r + n] = z16

    lane8 = lax.broadcasted_iota(jnp.int32, (8, BC), 1)
    top_tile = TILES - 1
    units = [(u // PER, u % PER) for u in range(16)]

    def put(tile, i, items, skip):
        left = right = None
        for u, (field, layer) in enumerate(items):
            x = fa[field, layer, pl.ds(pl.multiple_of(8 * i + OFF, 8), 8), :]
            x_l, x_r = turn(x, UNIT * u - skip), turn(x, UNIT * u + UNIT + skip)
            left = x_l if u == 0 else jnp.where(lane8 >= UNIT * u, x_l, left)
            right = x_r if u == 0 else jnp.where(lane8 >= UNIT * u, x_r, right)
        at = pl.ds(pl.multiple_of(8 * i, 8), 8)
        sl[tile, at, :] = left
        sr[tile, at, :] = right

    def pack_near(i, carry):
        for tile in (STIFF, LOAD):
            put(tile, i, [(tile, 1 + PER * t + s) for s, t in units], 0)
        return carry

    def pack_far(i, carry):
        put(2, i, [(t // 2, 1 + PER * top_tile * (t % 2) + s) for s, t in units], UNIT)
        put(3, i, [(PAIRS, k) for k in range(8)], 0)
        return carry

    for c in locals_[:2]:
        c.wait()
    lax.fori_loop(0, BR // 8, pack_near, 0)
    pl.semaphore_wait(barrier, NPEER - 1 + 2)

    count = [0]

    def send(src, dst, dev):
        n = count[0]
        count[0] += 1
        c = pltpu.make_async_remote_copy(src, dst, rs.at[n], rr.at[n], device_id=dev, device_id_type=MESH)
        c.start()
        return c

    near = []
    two = pl.ds(0, 2)
    ways = ((sl, mr, gym), (sr, ml, gyp))
    for buf, dst, dev_y in ways:
        near.append(send(buf.at[two], dst.at[two, own_rows, :], (body, gx, dev_y)))
    sides = (
        ((body, gxm, gy), OFF, OFF + BR, OFF + 8),
        ((body, gxp, gy), OFF + BR - 8, NLO, OFF + BR - 16),
    )
    layers = pl.ds(1, CZ)
    for dev, row, to, _ in sides:
        near.append(send(fa.at[two, layers, pl.ds(row, 8), :], fa.at[two, layers, pl.ds(to, 8), :], dev))
    for buf, dst, dev_y in ways:
        near.append(send(buf.at[two, pl.ds(0, 8), :], dst.at[two, pl.ds(OFF + BR, 8), :], (body, gxm, dev_y)))
        near.append(send(buf.at[two, pl.ds(BR - 8, 8), :], dst.at[two, pl.ds(NLO, 8), :], (body, gxp, dev_y)))

    for c in locals_[2:]:
        c.wait()
    for k in range(4):
        fa[PAIRS, k, OFF : OFF + BR] = ci[k].astype(F32)
    lax.fori_loop(0, BR // 8, pack_far, 0)
    late = []
    rest = pl.ds(2, 2)
    for buf, dst, dev_y in ways:
        late.append(send(buf.at[rest], dst.at[rest, own_rows, :], (body, gx, dev_y)))
        late.append(send(buf.at[rest, pl.ds(0, 16), :], dst.at[rest, pl.ds(OFF + BR, 16), :], (body, gxm, dev_y)))
        late.append(send(buf.at[rest, pl.ds(BR - 16, 16), :], dst.at[rest, pl.ds(LO, 16), :], (body, gxp, dev_y)))
        late.append(send(buf.at[two, pl.ds(8, 8), :], dst.at[two, pl.ds(NHI, 8), :], (body, gxm, dev_y)))
        late.append(send(buf.at[two, pl.ds(BR - 16, 8), :], dst.at[two, pl.ds(LO, 8), :], (body, gxp, dev_y)))
    pairs = pl.ds(0, 8)
    for side, (dev, row, to, far_row) in enumerate(sides):
        late.append(send(fa.at[two, layers, pl.ds(far_row, 8), :], far.at[side], dev))
        late.append(send(fa.at[PAIRS, pairs, pl.ds(row, 8), :], fa.at[PAIRS, pairs, pl.ds(to, 8), :], dev))

    def clear(l, carry):
        for r, n in chunks(0, BR, step):
            ifl[l, r : r + n] = z16
        return carry

    lax.fori_loop(1, CZ - 1, clear, 0)

    def entry(x_ref, lead, c, r, n):
        rows = slice(r, r + n)
        x = jnp.zeros((n, BC), F32)
        for k in range(4):
            x = x + jnp.where(x_ref[lead + (k, rows)] == c.astype(F32), x_ref[lead + (4 + k, rows)], 0.0)
        return x

    def own_table(c, carry):
        for r, n in chunks(OFF, OFF + BR, step):
            ta[c, r : r + n] = entry(fa, (PAIRS,), c, r, n)
        return carry

    lane16 = lax.broadcasted_iota(jnp.int32, (step, BC), 1)
    first, last = lane16 == 0, lane16 == BC - 1
    lane_ok = jnp.where(lane16 < BC // 2, right_ok, left_ok)
    in_slot = lax.bitwise_and(lane16, SLOT - 1)
    slot_ok = jnp.where(in_slot < HALF, left_ok, right_ok)
    is_l0, is_r0 = in_slot == HALF - 1, in_slot == HALF
    near_l = (in_slot >= UNIT) & (in_slot < HALF)
    near_r = (in_slot >= HALF) & (in_slot < HALF + UNIT)
    far_l, far_r = in_slot < UNIT, in_slot >= SLOT - UNIT
    low_slot, high_slot = lane16 < SLOT, lane16 >= BC - SLOT

    def row_ok_of(r):
        return top_ok if r < OFF else bot_ok if r >= OFF + BR else None

    def segments(lo, hi):
        return chunks(lo, OFF, step) + chunks(OFF, OFF + BR, step) + chunks(OFF + BR, hi, step)

    def fold(x):
        return jnp.sum(x.reshape(x.shape[0] // 8, 8, BC), axis=0)

    def masked(x, r, n):
        ok = row_ok_of(r)
        x = x * slot_ok[:n]
        return x if ok is None else x * ok

    def columns(tile, t, r, n):
        rows = slice(r, r + n)
        x = jnp.where(near_r[:n], turn(mr[tile, rows], HALF - UNIT * t), 0.0)
        return jnp.where(near_l[:n], turn(ml[tile, rows], UNIT - UNIT * t), x)

    lax.fori_loop(0, SPAN * SPAN, own_table, 0)
    for c in near:
        c.wait_recv()

    def unpack(i, carry):
        tile, t = i // TILES, lax.rem(i, TILES)
        for r, n in segments(NLO, NHI):
            fp[tile, t + 1, r : r + n] = masked(columns(tile, t, r, n), r, n)
        return carry

    def mask_rows(l, carry):
        fa[LOAD, l, NLO:OFF] = fa[LOAD, l, NLO:OFF] * top_ok
        fa[LOAD, l, OFF + BR : NHI] = fa[LOAD, l, OFF + BR : NHI] * bot_ok
        return carry

    lax.fori_loop(0, 2 * TILES, unpack, 0)
    lax.fori_loop(1, CZ + 1, mask_rows, 0)

    def image_a(p, k, l, r, n):
        rows = slice(r, r + n)
        a = fa[k, l, rows]
        s = turn(jnp.where(last[:n], p, a), 1) + turn(jnp.where(first[:n], p, a), -1)
        s = s + (fa[k, l, r - 1 : r - 1 + n] + fa[k, l, r + 1 : r + 1 + n])
        s = s + (fa[k, l - 1, rows] + fa[k, l + 1, rows])
        out = fa[STIFF, l, rows] * a - s
        ok = row_ok_of(r)
        return a, out if ok is None else out * ok

    def image_p(own, k, t, r, n):
        edge = None
        for s in range(PER):
            x = turn(own[s], SLOT * s + HALF)
            edge = x if s == 0 else jnp.where(lane16[:n] >= SLOT * s, x, edge)
        rows = slice(r, r + n)
        p = fp[k, t + 1, rows]
        s = turn(jnp.where(is_l0[:n], edge, p), 1) + turn(jnp.where(is_r0[:n], edge, p), -1)
        s = s + (fp[k, t + 1, r - 1 : r - 1 + n] + fp[k, t + 1, r + 1 : r + 1 + n])
        s = s + turn(jnp.where(high_slot[:n], fp[k, t, rows], p), SLOT)
        s = s + turn(jnp.where(low_slot[:n], fp[k, t + 2, rows], p), -SLOT)
        return masked(fp[STIFF, t + 1, rows] * p - s, r, n)

    row_lane = lax.broadcasted_iota(jnp.int32, (1, BC), 1)

    def others(n):
        return mbuf.at[n, pl.ds(0, NPEER - 1)]

    def relays(n):
        return [
            pltpu.make_async_remote_copy(
                mz.at[n, 2], mz.at[n, side], zs.at[n, side], zr.at[n, side],
                device_id=(dev, gx, gy), device_id_type=MESH,
            )
            for side, dev in ((0, above), (1, below))
        ]

    def faces(n, which):
        k0 = pl.ds(LOAD + 4 * n, 3)

        def part(to, size):
            return fa.at[k0, 1, pl.ds(NLO + to, size), :], got.at[n, 0, pl.ds(0, 3), pl.ds(to, size), :]

        far_part = NHI - NLO - 8
        pairs_ = (
            (stage.at[n], got.at[n, 1], above),
            (*part(8, BR), below),
            (*part(0, 8), below),
            (*part(far_part, 8), below),
            (stage_low.at[n], got.at[n, 0, 3], below),
        )
        return [
            pltpu.make_async_remote_copy(
                x, y, fs.at[n, i], fr.at[n, i], device_id=(dev, gx, gy), device_id_type=MESH
            )
            for i, (x, y, dev) in enumerate(pairs_)
            if i in which
        ]

    def side_columns(k0, t, slot, r, cnt):
        x = None
        for k in range(3):
            y = turn(fp[k0 + k, t, r : r + cnt], SLOT * (k - slot))
            x = y if k == 0 else jnp.where(lane16[:cnt] >= SLOT * k, y, x)
        return x

    def send_early(n):
        k0 = LOAD + 4 * n
        for r, cnt in chunks(NLO, NHI, step):
            at = slice(r - NLO, r - NLO + cnt)
            for k in range(3):
                stage[n, k, at] = fa[k0 + k, CZ, r : r + cnt]
            stage[n, 3, at] = side_columns(k0, TILES, PER - 1, r, cnt)
        for c in faces(n, (0, 1)):
            c.start()

    def send_rest(n):
        k0 = LOAD + 4 * n
        for r, cnt in chunks(NLO, NHI, step):
            stage_low[n, r - NLO : r - NLO + cnt] = side_columns(k0, 1, 0, r, cnt)
        for c in faces(n, (2, 3, 4)):
            c.start()

    def coefficients(total, where):
        m = [jnp.sum(jnp.where(row_lane == k, total, 0.0), axis=1, keepdims=True) for k in range(6)]
        h = [m[k + 1] + SHIFT * m[k] for k in range(5)]
        inv = 1.0 / h[0]
        l10, l20 = h[1] * inv, h[2] * inv
        d1 = h[2] - l10 * h[1]
        e12 = h[3] - l20 * h[1]
        inv1 = 1.0 / d1
        l21 = e12 * inv1
        d2 = h[4] - l20 * h[2] - l21 * e12
        y1 = m[1] - l10 * m[0]
        y2 = m[2] - l20 * m[0] - l21 * y1
        c2 = y2 / d2
        c1 = y1 * inv1 - l21 * c2
        c0 = m[0] * inv - l10 * c1 - l20 * c2
        for k, c in enumerate((c0, c1, c2)):
            co[where, k] = jnp.broadcast_to(c, (step, BC))

    def combine(ref, k0, where, l, r, n):
        rows = slice(r, r + n)
        x = [co[where, k][:n] * ref[k0 + k, l, rows] for k in range(3)]
        return (x[0] + x[1]) + x[2]

    def moved(a, b, by):
        at = lane16[: a.shape[0]] - by
        late_ = (at < 0) | (at > BC - 1)
        return turn(jnp.where(late_, b, a), -by), turn(jnp.where(late_, a, b), -by)

    inner = chunks(NLO, NHI, step)
    block = chunks(OFF, OFF + BR, step)

    def nothing(pieces):
        return tuple(jnp.zeros((n, BC), F32) for _, n in pieces)

    def pull(side, pieces=inner, beside=True):
        def one(d, sums):
            xs, ys = sums
            for r, n in chunks(LO, HI, step):
                rows = slice(r, r + n)
                sha[rows], shb[rows] = moved(face[side, rows], side_face[side, rows], d - REACH)
            out_x, out_y = [], []
            for (r, n), x, y in zip(pieces, xs, ys):
                for dx in range(SPAN):
                    c, q = dx * SPAN + d, r + dx - REACH
                    x = x + ta[c, r : r + n] * sha[q : q + n]
                    if beside:
                        y = y + tb[c, r : r + n] * shb[q : q + n]
                out_x.append(x)
                out_y.append(y)
            return tuple(out_x), tuple(out_y)

        return lax.fori_loop(0, SPAN, one, (nothing(pieces), nothing(pieces)))

    def push(pieces):
        def one(d, sums):
            xs, ys = sums
            out_x, out_y = [], []
            for (r, n), x, y in zip(pieces, xs, ys):
                p = q = jnp.zeros((n, BC), F32)
                for dx in range(SPAN):
                    c, o = dx * SPAN + d, r - dx + REACH
                    p = p + ta[c, o : o + n] * mult[0, o : o + n]
                    q = q + tb[c, o : o + n] * mult[1, o : o + n]
                p, q = moved(p, q, REACH - d)
                out_x.append(x + p)
                out_y.append(y + q)
            return tuple(out_x), tuple(out_y)

        return lax.fori_loop(0, SPAN, one, (nothing(pieces), nothing(pieces)))

    def far_tier():
        for c in late:
            c.wait_recv()

        def rows_in(l, carry):
            for side, (r, ok) in enumerate(((NHI, bot_ok), (LO, top_ok))):
                for k in range(2):
                    fa[k, l + 1, r : r + 8] = far[side, k, l] * ok
            return carry

        def columns_in(i, carry):
            tile, f = i // 2, lax.rem(i, 2)
            g = f + 2 * tile
            t = top_tile * f
            for r, n in segments(LO, HI):
                rows = slice(r, r + n)
                x = jnp.where(far_r[:n], turn(mr[2, rows], SLOT - UNIT - UNIT * g), columns(tile, t, r, n))
                x = jnp.where(far_l[:n], turn(ml[2, rows], -UNIT * g), x)
                fp[tile, t + 1, rows] = masked(x, r, n)
            return carry

        lax.fori_loop(0, CZ, rows_in, 0)
        lax.fori_loop(0, 4, columns_in, 0)

        def again(k, carry):
            def layer(i, carry):
                l = jnp.where(i < 2, i, i + 11)
                t, s = l // PER, lax.rem(l, PER)
                for r in (LO, OFF + BR):
                    p = turn(fp[k, t + 1, r : r + step], -(SLOT * s + HALF))
                    fa[k + 1, l + 1, r : r + step] = image_a(p, k, l + 1, r, step)[1]
                return carry

            def tile(i, carry):
                t = top_tile * i
                for r, n in segments(LO, HI):
                    own = [fa[k, PER * t + s + 1, r : r + n] for s in range(PER)]
                    fp[k + 1, t + 1, r : r + n] = image_p(own, k, t, r, n)
                return carry

            lax.fori_loop(0, 5, layer, 0)
            lax.fori_loop(0, 2, tile, 0)
            return carry

        lax.fori_loop(LOAD, LOAD + 3, again, 0)

    def side_pairs():
        def mask(k, carry):
            fa[PAIRS, k, NLO:OFF] = fa[PAIRS, k, NLO:OFF] * top_ok
            fa[PAIRS, k, OFF + BR : NHI] = fa[PAIRS, k, OFF + BR : NHI] * bot_ok
            return carry

        lax.fori_loop(4, 8, mask, 0)

        def beside(u, carry):
            for r, n in segments(NLO, NHI):
                rows = slice(r, r + n)
                ok = row_ok_of(r)
                ok = lane_ok[:n] if ok is None else lane_ok[:n] * ok
                x = jnp.where(lane16[:n] >= BC - UNIT, turn(ml[3, rows], BC - UNIT - UNIT * u), 0.0)
                x = jnp.where(lane16[:n] < UNIT, turn(mr[3, rows], -UNIT * u), x)
                cb[u, rows] = jnp.where(u < 4, x, x * ok)
            return carry

        lax.fori_loop(0, 8, beside, 0)

    def outer_table(c, carry):
        for r in (NLO, OFF + BR):
            ta[c, r : r + 8] = entry(fa, (PAIRS,), c, r, 8)
        for r, n in inner:
            tb[c, r : r + n] = entry(cb, (), c, r, n)
        return carry


    def zero_sums():
        for k in range(6):
            acc[k] = z8

    def powers(k0, count, which, keep=True):
        def one(i, carry):
            j, t = which(i)
            k = k0 + j
            acc0 = acc1 = jnp.zeros((8, BC), F32)
            for r, cnt in segments(NLO, NHI) if keep else chunks(OFF, OFF + BR, step):
                p = fp[k, t + 1, r : r + cnt]
                own = []
                for s in range(PER):
                    l = PER * t + s + 1
                    a, out = image_a(turn(p, -(SLOT * s + HALF)), k, l, r, cnt)
                    own.append(a)
                    if row_ok_of(r) is None:
                        acc0 = acc0 + fold(a * a)
                        acc1 = acc1 + fold(a * out)
                    if keep:
                        fa[k + 1, l, r : r + cnt] = out
                if keep:
                    fp[k + 1, t + 1, r : r + cnt] = image_p(own, k, t, r, cnt)
            acc[2 * j] = acc[2 * j] + acc0
            acc[2 * j + 1] = acc[2 * j + 1] + acc1
            return carry

        lax.fori_loop(0, count, one, 0)

    def update(n, carry):
        k0 = LOAD + 4 * n
        if n == 0:
            zero_sums()
            powers(k0, 3 * TILES, lambda i: (lax.div(i, TILES), lax.rem(i, TILES)))
        else:
            powers(
                k0,
                2 + TILES,
                lambda i: (jnp.where(i < 2, 0, 1), jnp.where(i < 2, top_tile * i, i - 2)),
            )
            powers(k0, TILES, lambda i: (2, i), keep=False)

        row = jnp.zeros((1, BC), F32)
        for k in range(6):
            row = row + jnp.where(row_lane == k, jnp.sum(acc[k], keepdims=True), 0.0)
        mrow[n, 0] = row
        mbuf[n, me] = row

        def go(i, carry):
            pltpu.make_async_remote_copy(
                mrow.at[n, 0], mbuf.at[n, me], as_.at[n], ar.at[n], device_id=peer(i), device_id_type=MESH
            ).start()
            return carry

        lax.fori_loop(0, NPEER - 1, go, 0)

        send_early(n)
        when(n == 0)(far_tier)
        send_rest(n)
        when(n == 0)(side_pairs)

        pltpu.make_async_copy(others(n), others(n), ar.at[n]).wait()
        total = jnp.sum(mbuf[n], axis=0)
        mz[n, 2] = total
        for c in relays(n):
            c.start()
        coefficients(total, n)

        @when(n == 0)
        def _():
            def residual(t, carry):
                c = [co[0, k] for k in range(3)]
                g = [1.0 - SHIFT * c[0], -(c[0] + SHIFT * c[1]), -(c[1] + SHIFT * c[2]), -c[2]]
                for r, cnt in inner:
                    rows = slice(r, r + cnt)
                    for ref, l in [(fp, t + 1)] + [(fa, PER * t + s + 1) for s in range(PER)]:
                        x = [g[k][:cnt] * ref[LOAD + k, l, rows] for k in range(4)]
                        ref[LOAD + 4, l, rows] = (x[0] + x[1]) + (x[2] + x[3])
                return carry

            lax.fori_loop(0, TILES, residual, 0)
            lax.fori_loop(0, SPAN * SPAN, outer_table, 0)

        @when(n == 1)
        def _():
            def answer(l, carry):
                for r, cnt in chunks(OFF, OFF + BR, step):
                    x = combine(fa, LOAD, 0, l, r, cnt) + combine(fa, LOAD + 4, 1, l, r, cnt)
                    sol[l - 1, r - OFF : r - OFF + cnt] = x
                return carry

            lax.fori_loop(1, CZ + 1, answer, 0)

        for r, cnt in chunks(LO, HI, step):
            face[0, r : r + cnt] = combine(fa, k0, n, CZ, r, cnt)
            side_face[0, r : r + cnt] = turn(combine(fp, k0, n, TILES, r, cnt), HALF)

        for (r, cnt), x, y in zip(inner, *pull(0)):
            face[0, r : r + cnt] = x
            side_face[0, r : r + cnt] = y
        if n == 0:
            zero_sums()
            powers(LOAD + 4, TILES - 2, lambda i: (0, i + 1))

        for c in relays(n) + faces(n, range(5)):
            c.wait()

        def solve(side, carry):
            coefficients(mz[n, side], 2 + side)
            return carry

        lax.fori_loop(0, 2, solve, 0)

        def from_body(side, where, r, cnt):
            at = slice(r - NLO, r - NLO + cnt)
            c = [co[where, k][:cnt] for k in range(3)]
            x = [c[k] * got[n, side, k, at] for k in range(3)]
            packed = got[n, side, 3, at]
            y = [c[k] * turn(packed, -(SLOT * k + HALF)) for k in range(3)]
            return (x[0] + x[1]) + x[2], (y[0] + y[1]) + y[2]

        for r in (LO, NHI):
            face[1, r : r + 8] = z8
            side_face[1, r : r + 8] = z8
        for r, cnt in inner:
            rows = slice(r, r + cnt)
            face[1, rows], side_face[1, rows] = from_body(1, 2, r, cnt)

        pieces = inner if n == 0 else block
        for (r, cnt), x, y in zip(pieces, *pull(1, pieces, n == 0)):
            face[1, r : r + cnt] = x
            side_face[1, r : r + cnt] = y

        for r, cnt in inner:
            rows = slice(r, r + cnt)
            x, y = from_body(0, 3, r, cnt)
            mult[0, rows] = 2.0 * mult[0, rows] + scale_up * (x - face[0, rows])
            mult[1, rows] = 2.0 * mult[1, rows] + scale_up * (y - side_face[0, rows])
            x = scale_dn * (combine(fa, k0, n, 1, r, cnt) - face[1, rows])
            low[rows] = 2.0 * low[rows] + x
        for (r, cnt), x, y in zip(pieces, *push(pieces)):
            force[0, r : r + cnt] = x
            if n == 0:
                force[1, r : r + cnt] = y

        @when(n == 0)
        def _():
            for r, cnt in segments(NLO, NHI):
                rows = slice(r, r + cnt)
                ok = row_ok_of(r)
                x, y = force[0, rows], force[1, rows] * lane_ok[:cnt]
                if ok is not None:
                    x, y = x * ok, y * ok
                fa[LOAD + 4, CZ, rows] = fa[LOAD + 4, CZ, rows] + x
                back = jnp.where(high_slot[:cnt], turn(y, -HALF), 0.0)
                fp[LOAD + 4, TILES, rows] = fp[LOAD + 4, TILES, rows] + back
                fa[LOAD + 4, 1, rows] = fa[LOAD + 4, 1, rows] - low[rows]
                y = scale_dn * (turn(combine(fp, LOAD, 0, 1, r, cnt), -HALF) - side_face[1, rows])
                back = jnp.where(low_slot[:cnt], turn(y, HALF), 0.0)
                fp[LOAD + 4, 1, rows] = fp[LOAD + 4, 1, rows] - back

        return carry

    update(0, 0)
    update(1, 0)

    for r, n in chunks(OFF, OFF + BR, step):
        ifl[CZ - 1, r - OFF : r - OFF + n] = force[0, r : r + n]
        ifl[0, r - OFF : r - OFF + n] = -low[r : r + n]
    for c in near + late:
        c.wait_send()
    for n in range(2):
        pltpu.make_async_copy(others(n), others(n), as_.at[n]).wait()


def per_device(load, stiffness, pair_code, pair_weight):
    def plane(*lead):
        return pltpu.VMEM((*lead, ROWS, BC), F32)

    def vmem(*shape):
        return pltpu.VMEM((*shape, BC), F32)

    dma = pltpu.SemaphoreType.DMA
    nsend, near = 22, NHI - NLO
    scratch = [
        plane(10, CZ + 2), plane(10, TILES + 2), pltpu.VMEM((4, BR, BC), jnp.int32), plane(8),
        vmem(4, BR), vmem(4, BR), plane(4), plane(4), vmem(2, 2, CZ, 8),
        plane(SPAN * SPAN), plane(SPAN * SPAN), plane(), plane(), plane(2), plane(2), plane(2), plane(), plane(2),
        vmem(2, 4, near), vmem(2, near), vmem(2, 2, 4, near), vmem(6, 8), vmem(4, 3, 16),
        vmem(2, 1, 1), vmem(2, NPEER, 1), vmem(2, 3, 1),
        dma((4,)), dma((nsend,)), dma((nsend,)), dma((2, 5)), dma((2, 5)),
        dma((2,)), dma((2,)), dma((2, 2)), dma((2, 2)),
    ]
    return pl.pallas_call(
        kernel,
        out_shape=(pltpu.VMEM((CZ, BR, BC), F32),) * 2,
        in_specs=[pl.BlockSpec(memory_space=pl.ANY)] * 4,
        out_specs=[pl.BlockSpec(memory_space=pltpu.VMEM)] * 2,
        scratch_shapes=scratch,
        compiler_params=pltpu.CompilerParams(collective_id=0, has_side_effects=True),
        name="uzawa",
    )(load, stiffness, pair_code, pair_weight)


def solution(mesh):
    return jax.shard_map(
        per_device,
        mesh=mesh,
        in_specs=(
            P("body", "gx", "gy"),
            P("body", "gx", "gy"),
            P(None, "gx", "gy"),
            P(None, "gx", "gy"),
        ),
        out_specs=(P("body", "gx", "gy"), P("body", "gx", "gy")),
        check_vma=False,
    )
```

```python
import jax
import jax.numpy as jnp
from jax import lax
from jax.experimental import pallas as pl
from jax.experimental.pallas import tpu as pltpu
from jax.sharding import PartitionSpec as P

MESH = pl.DeviceIdType.MESH
F32 = jnp.float32

NBODY, NGX, NGY = 8, 8, 4
NPEER = NGX * NGY
CZ, BR, BC = 16, 64, 128
REACH, SPAN, RATE = 2, 5, 2.0
OFF = 24
ROWS = BR + 2 * OFF
LO, HI = 8, ROWS - 8
NLO, NHI = 16, ROWS - 16
SLOT, HALF = 32, 16
PER = BC // SLOT
TILES = CZ // PER
UNIT = 8
SHIFT = 6.0
STIFF, LOAD, PAIRS = 0, 1, 9


def turn(x, by):
    if isinstance(by, int):
        by %= BC
        return x if by == 0 else pltpu.roll(x, by, x.ndim - 1)
    return pltpu.roll(x, lax.rem(by + BC, BC), x.ndim - 1)


def when(flag):
    return lambda f: f() if flag else None


def chunks(first, last, step):
    return [(r, min(step, last - r)) for r in range(first, last, step)]


def kernel(
    load, stiff, code, weight, sol, ifl,
    fa, fp, ci, cb, sl, sr, ml, mr, far, ta, tb, sha, shb, face, side_face, mult, low, force,
    stage, stage_low, got, acc, co, mrow, mbuf, mz,
    lsem, rs, rr, fs, fr, as_, ar, zs, zr,
):
    body, gx, gy = (lax.axis_index(n) for n in ("body", "gx", "gy"))
    me = gx * NGY + gy
    gxm, gxp = lax.rem(gx + NGX - 1, NGX), lax.rem(gx + 1, NGX)
    gym, gyp = lax.rem(gy + NGY - 1, NGY), lax.rem(gy + 1, NGY)
    below, above = lax.rem(body + NBODY - 1, NBODY), lax.rem(body + 1, NBODY)

    def peer(i):
        o = i + 12
        o = jnp.where(o >= NPEER, o - (NPEER - 1), o)
        p = me + o
        p = jnp.where(p >= NPEER, p - NPEER, p)
        return (body, lax.div(p, NGY), lax.rem(p, NGY))

    barrier = pltpu.get_barrier_semaphore()

    def greet(i, carry):
        pl.semaphore_signal(barrier, inc=1, device_id=peer(i), device_id_type=MESH)
        return carry

    own_rows = pl.ds(OFF, BR)
    locals_ = [
        pltpu.make_async_copy(stiff, fa.at[STIFF, pl.ds(1, CZ), own_rows, :], lsem.at[0]),
        pltpu.make_async_copy(load, fa.at[LOAD, pl.ds(1, CZ), own_rows, :], lsem.at[1]),
        pltpu.make_async_copy(code, ci, lsem.at[2]),
        pltpu.make_async_copy(weight, fa.at[PAIRS, pl.ds(4, 4), own_rows, :], lsem.at[3]),
    ]
    for c in locals_:
        c.start()
    lax.fori_loop(0, NPEER - 1, greet, 0)
    pl.semaphore_signal(barrier, inc=1, device_id=(below, gx, gy), device_id_type=MESH)
    pl.semaphore_signal(barrier, inc=1, device_id=(above, gx, gy), device_id_type=MESH)

    one = jnp.float32(1.0)
    zero = jnp.float32(0.0)
    top_ok = jnp.where(gx > 0, one, zero)
    bot_ok = jnp.where(gx < NGX - 1, one, zero)
    right_ok = jnp.where(gy < NGY - 1, one, zero)
    left_ok = jnp.where(gy > 0, one, zero)
    scale_up = jnp.where(body < NBODY - 1, jnp.float32(RATE), zero)
    scale_dn = jnp.where(body > 0, jnp.float32(RATE), zero)

    step = 16
    z16 = jnp.zeros((step, BC), F32)
    z8 = jnp.zeros((8, BC), F32)

    def zero_ends(i, carry):
        for r, n in chunks(0, ROWS, step):
            for l in (0, CZ + 1):
                fa[i + LOAD, l, r : r + n] = z16
            for t in (0, TILES + 1):
                fp[i + LOAD, t, r : r + n] = z16
        return carry

    def zero_far(l, carry):
        for r in (LO, NHI):
            for k in range(4):
                fa[k, l, r : r + 8] = z8
        return carry

    lax.fori_loop(0, 8, zero_ends, 0)
    lax.fori_loop(1, CZ + 1, zero_far, 0)
    for k in range(2):
        for r in (LO, NHI):
            mult[k, r : r + 8] = z8
            for t in range(TILES):
                fp[k, t + 1, r : r + 8] = z8
        for r, n in chunks(NLO, NHI, step):
            mult[k, r : r + n] = z16
    for r, n in chunks(NLO, NHI, step):
        low[r : r + n] = z16

    lane8 = lax.broadcasted_iota(jnp.int32, (8, BC), 1)
    top_tile = TILES - 1
    units = [(u // PER, u % PER) for u in range(16)]

    def put(tile, i, items, skip):
        left = right = None
        for u, (field, layer) in enumerate(items):
            x = fa[field, layer, pl.ds(pl.multiple_of(8 * i + OFF, 8), 8), :]
            x_l, x_r = turn(x, UNIT * u - skip), turn(x, UNIT * u + UNIT + skip)
            left = x_l if u == 0 else jnp.where(lane8 >= UNIT * u, x_l, left)
            right = x_r if u == 0 else jnp.where(lane8 >= UNIT * u, x_r, right)
        at = pl.ds(pl.multiple_of(8 * i, 8), 8)
        sl[tile, at, :] = left
        sr[tile, at, :] = right

    def pack_near(i, carry):
        for tile in (STIFF, LOAD):
            put(tile, i, [(tile, 1 + PER * t + s) for s, t in units], 0)
        return carry

    def pack_far(i, carry):
        put(2, i, [(t // 2, 1 + PER * top_tile * (t % 2) + s) for s, t in units], UNIT)
        put(3, i, [(PAIRS, k) for k in range(8)], 0)
        return carry

    for c in locals_[:2]:
        c.wait()
    lax.fori_loop(0, BR // 8, pack_near, 0)
    pl.semaphore_wait(barrier, NPEER - 1 + 2)

    count = [0]

    def send(src, dst, dev):
        n = count[0]
        count[0] += 1
        c = pltpu.make_async_remote_copy(src, dst, rs.at[n], rr.at[n], device_id=dev, device_id_type=MESH)
        c.start()
        return c

    near = []
    two = pl.ds(0, 2)
    ways = ((sl, mr, gym), (sr, ml, gyp))
    for buf, dst, dev_y in ways:
        near.append(send(buf.at[two], dst.at[two, own_rows, :], (body, gx, dev_y)))
    sides = (
        ((body, gxm, gy), OFF, OFF + BR, OFF + 8),
        ((body, gxp, gy), OFF + BR - 8, NLO, OFF + BR - 16),
    )
    layers = pl.ds(1, CZ)
    for dev, row, to, _ in sides:
        near.append(send(fa.at[two, layers, pl.ds(row, 8), :], fa.at[two, layers, pl.ds(to, 8), :], dev))
    for buf, dst, dev_y in ways:
        near.append(send(buf.at[two, pl.ds(0, 8), :], dst.at[two, pl.ds(OFF + BR, 8), :], (body, gxm, dev_y)))
        near.append(send(buf.at[two, pl.ds(BR - 8, 8), :], dst.at[two, pl.ds(NLO, 8), :], (body, gxp, dev_y)))

    for c in locals_[2:]:
        c.wait()
    for k in range(4):
        fa[PAIRS, k, OFF : OFF + BR] = ci[k].astype(F32)
    lax.fori_loop(0, BR // 8, pack_far, 0)
    late = []
    rest = pl.ds(2, 2)
    for buf, dst, dev_y in ways:
        late.append(send(buf.at[rest], dst.at[rest, own_rows, :], (body, gx, dev_y)))
        late.append(send(buf.at[rest, pl.ds(0, 16), :], dst.at[rest, pl.ds(OFF + BR, 16), :], (body, gxm, dev_y)))
        late.append(send(buf.at[rest, pl.ds(BR - 16, 16), :], dst.at[rest, pl.ds(LO, 16), :], (body, gxp, dev_y)))
        late.append(send(buf.at[two, pl.ds(8, 8), :], dst.at[two, pl.ds(NHI, 8), :], (body, gxm, dev_y)))
        late.append(send(buf.at[two, pl.ds(BR - 16, 8), :], dst.at[two, pl.ds(LO, 8), :], (body, gxp, dev_y)))
    pairs = pl.ds(0, 8)
    for side, (dev, row, to, far_row) in enumerate(sides):
        late.append(send(fa.at[two, layers, pl.ds(far_row, 8), :], far.at[side], dev))
        late.append(send(fa.at[PAIRS, pairs, pl.ds(row, 8), :], fa.at[PAIRS, pairs, pl.ds(to, 8), :], dev))

    def clear(l, carry):
        for r, n in chunks(0, BR, step):
            ifl[l, r : r + n] = z16
        return carry

    lax.fori_loop(1, CZ - 1, clear, 0)

    def entry(x_ref, lead, c, r, n):
        rows = slice(r, r + n)
        x = jnp.zeros((n, BC), F32)
        for k in range(4):
            x = x + jnp.where(x_ref[lead + (k, rows)] == c.astype(F32), x_ref[lead + (4 + k, rows)], 0.0)
        return x

    def own_table(c, carry):
        for r, n in chunks(OFF, OFF + BR, step):
            ta[c, r : r + n] = entry(fa, (PAIRS,), c, r, n)
        return carry

    lane16 = lax.broadcasted_iota(jnp.int32, (step, BC), 1)
    first, last = lane16 == 0, lane16 == BC - 1
    lane_ok = jnp.where(lane16 < BC // 2, right_ok, left_ok)
    in_slot = lax.bitwise_and(lane16, SLOT - 1)
    slot_ok = jnp.where(in_slot < HALF, left_ok, right_ok)
    is_l0, is_r0 = in_slot == HALF - 1, in_slot == HALF
    near_l = (in_slot >= UNIT) & (in_slot < HALF)
    near_r = (in_slot >= HALF) & (in_slot < HALF + UNIT)
    far_l, far_r = in_slot < UNIT, in_slot >= SLOT - UNIT
    low_slot, high_slot = lane16 < SLOT, lane16 >= BC - SLOT

    def row_ok_of(r):
        return top_ok if r < OFF else bot_ok if r >= OFF + BR else None

    def segments(lo, hi):
        return chunks(lo, OFF, step) + chunks(OFF, OFF + BR, step) + chunks(OFF + BR, hi, step)

    def fold(x):
        return jnp.sum(x.reshape(x.shape[0] // 8, 8, BC), axis=0)

    def masked(x, r, n):
        ok = row_ok_of(r)
        x = x * slot_ok[:n]
        return x if ok is None else x * ok

    def columns(tile, t, r, n):
        rows = slice(r, r + n)
        x = jnp.where(near_r[:n], turn(mr[tile, rows], HALF - UNIT * t), 0.0)
        return jnp.where(near_l[:n], turn(ml[tile, rows], UNIT - UNIT * t), x)

    lax.fori_loop(0, SPAN * SPAN, own_table, 0)
    for c in near:
        c.wait_recv()

    def unpack(i, carry):
        tile, t = i // TILES, lax.rem(i, TILES)
        for r, n in segments(NLO, NHI):
            fp[tile, t + 1, r : r + n] = masked(columns(tile, t, r, n), r, n)
        return carry

    def mask_rows(l, carry):
        fa[LOAD, l, NLO:OFF] = fa[LOAD, l, NLO:OFF] * top_ok
        fa[LOAD, l, OFF + BR : NHI] = fa[LOAD, l, OFF + BR : NHI] * bot_ok
        return carry

    lax.fori_loop(0, 2 * TILES, unpack, 0)
    lax.fori_loop(1, CZ + 1, mask_rows, 0)

    def image_a(p, k, l, r, n):
        rows = slice(r, r + n)
        a = fa[k, l, rows]
        s = turn(jnp.where(last[:n], p, a), 1) + turn(jnp.where(first[:n], p, a), -1)
        s = s + (fa[k, l, r - 1 : r - 1 + n] + fa[k, l, r + 1 : r + 1 + n])
        s = s + (fa[k, l - 1, rows] + fa[k, l + 1, rows])
        out = fa[STIFF, l, rows] * a - s
        ok = row_ok_of(r)
        return a, out if ok is None else out * ok

    def image_p(own, k, t, r, n):
        edge = None
        for s in range(PER):
            x = turn(own[s], SLOT * s + HALF)
            edge = x if s == 0 else jnp.where(lane16[:n] >= SLOT * s, x, edge)
        rows = slice(r, r + n)
        p = fp[k, t + 1, rows]
        s = turn(jnp.where(is_l0[:n], edge, p), 1) + turn(jnp.where(is_r0[:n], edge, p), -1)
        s = s + (fp[k, t + 1, r - 1 : r - 1 + n] + fp[k, t + 1, r + 1 : r + 1 + n])
        s = s + turn(jnp.where(high_slot[:n], fp[k, t, rows], p), SLOT)
        s = s + turn(jnp.where(low_slot[:n], fp[k, t + 2, rows], p), -SLOT)
        return masked(fp[STIFF, t + 1, rows] * p - s, r, n)

    row_lane = lax.broadcasted_iota(jnp.int32, (1, BC), 1)

    def others(n):
        return mbuf.at[n, pl.ds(0, NPEER - 1)]

    def relays(n):
        return [
            pltpu.make_async_remote_copy(
                mz.at[n, 2], mz.at[n, side], zs.at[n, side], zr.at[n, side],
                device_id=(dev, gx, gy), device_id_type=MESH,
            )
            for side, dev in ((0, above), (1, below))
        ]

    def faces(n, which):
        k0 = pl.ds(LOAD + 4 * n, 3)

        def part(to, size):
            return fa.at[k0, 1, pl.ds(NLO + to, size), :], got.at[n, 0, pl.ds(0, 3), pl.ds(to, size), :]

        far_part = NHI - NLO - 8
        pairs_ = (
            (stage.at[n], got.at[n, 1], above),
            (*part(8, BR), below),
            (*part(0, 8), below),
            (*part(far_part, 8), below),
            (stage_low.at[n], got.at[n, 0, 3], below),
        )
        return [
            pltpu.make_async_remote_copy(
                x, y, fs.at[n, i], fr.at[n, i], device_id=(dev, gx, gy), device_id_type=MESH
            )
            for i, (x, y, dev) in enumerate(pairs_)
            if i in which
        ]

    def side_columns(k0, t, slot, r, cnt):
        x = None
        for k in range(3):
            y = turn(fp[k0 + k, t, r : r + cnt], SLOT * (k - slot))
            x = y if k == 0 else jnp.where(lane16[:cnt] >= SLOT * k, y, x)
        return x

    def send_early(n):
        k0 = LOAD + 4 * n
        for r, cnt in chunks(NLO, NHI, step):
            at = slice(r - NLO, r - NLO + cnt)
            for k in range(3):
                stage[n, k, at] = fa[k0 + k, CZ, r : r + cnt]
            stage[n, 3, at] = side_columns(k0, TILES, PER - 1, r, cnt)
        for c in faces(n, (0, 1)):
            c.start()

    def send_rest(n):
        k0 = LOAD + 4 * n
        for r, cnt in chunks(NLO, NHI, step):
            stage_low[n, r - NLO : r - NLO + cnt] = side_columns(k0, 1, 0, r, cnt)
        for c in faces(n, (2, 3, 4)):
            c.start()

    def coefficients(total, where):
        m = [jnp.sum(jnp.where(row_lane == k, total, 0.0), axis=1, keepdims=True) for k in range(6)]
        h = [m[k + 1] + SHIFT * m[k] for k in range(5)]
        inv = 1.0 / h[0]
        l10, l20 = h[1] * inv, h[2] * inv
        d1 = h[2] - l10 * h[1]
        e12 = h[3] - l20 * h[1]
        inv1 = 1.0 / d1
        l21 = e12 * inv1
        d2 = h[4] - l20 * h[2] - l21 * e12
        y1 = m[1] - l10 * m[0]
        y2 = m[2] - l20 * m[0] - l21 * y1
        c2 = y2 / d2
        c1 = y1 * inv1 - l21 * c2
        c0 = m[0] * inv - l10 * c1 - l20 * c2
        for k, c in enumerate((c0, c1, c2)):
            co[where, k] = jnp.broadcast_to(c, (step, BC))

    def combine(ref, k0, where, l, r, n):
        rows = slice(r, r + n)
        x = [co[where, k][:n] * ref[k0 + k, l, rows] for k in range(3)]
        return (x[0] + x[1]) + x[2]

    def moved(a, b, by):
        at = lane16[: a.shape[0]] - by
        late_ = (at < 0) | (at > BC - 1)
        return turn(jnp.where(late_, b, a), -by), turn(jnp.where(late_, a, b), -by)

    inner = chunks(NLO, NHI, step)
    block = chunks(OFF, OFF + BR, step)

    def nothing(pieces):
        return tuple(jnp.zeros((n, BC), F32) for _, n in pieces)

    def pull(side, pieces=inner, beside=True):
        def one(d, sums):
            xs, ys = sums
            for r, n in chunks(LO, HI, step):
                rows = slice(r, r + n)
                sha[rows], shb[rows] = moved(face[side, rows], side_face[side, rows], d - REACH)
            out_x, out_y = [], []
            for (r, n), x, y in zip(pieces, xs, ys):
                for dx in range(SPAN):
                    c, q = dx * SPAN + d, r + dx - REACH
                    x = x + ta[c, r : r + n] * sha[q : q + n]
                    if beside:
                        y = y + tb[c, r : r + n] * shb[q : q + n]
                out_x.append(x)
                out_y.append(y)
            return tuple(out_x), tuple(out_y)

        return lax.fori_loop(0, SPAN, one, (nothing(pieces), nothing(pieces)))

    def push(pieces):
        def one(d, sums):
            xs, ys = sums
            out_x, out_y = [], []
            for (r, n), x, y in zip(pieces, xs, ys):
                p = q = jnp.zeros((n, BC), F32)
                for dx in range(SPAN):
                    c, o = dx * SPAN + d, r - dx + REACH
                    p = p + ta[c, o : o + n] * mult[0, o : o + n]
                    q = q + tb[c, o : o + n] * mult[1, o : o + n]
                p, q = moved(p, q, REACH - d)
                out_x.append(x + p)
                out_y.append(y + q)
            return tuple(out_x), tuple(out_y)

        return lax.fori_loop(0, SPAN, one, (nothing(pieces), nothing(pieces)))

    def far_tier():
        for c in late:
            c.wait_recv()

        def rows_in(l, carry):
            for side, (r, ok) in enumerate(((NHI, bot_ok), (LO, top_ok))):
                for k in range(2):
                    fa[k, l + 1, r : r + 8] = far[side, k, l] * ok
            return carry

        def columns_in(i, carry):
            tile, f = i // 2, lax.rem(i, 2)
            g = f + 2 * tile
            t = top_tile * f
            for r, n in segments(LO, HI):
                rows = slice(r, r + n)
                x = jnp.where(far_r[:n], turn(mr[2, rows], SLOT - UNIT - UNIT * g), columns(tile, t, r, n))
                x = jnp.where(far_l[:n], turn(ml[2, rows], -UNIT * g), x)
                fp[tile, t + 1, rows] = masked(x, r, n)
            return carry

        lax.fori_loop(0, CZ, rows_in, 0)
        lax.fori_loop(0, 4, columns_in, 0)

        def again(k, carry):
            def layer(i, carry):
                l = jnp.where(i < 2, i, i + 11)
                t, s = l // PER, lax.rem(l, PER)
                for r in (LO, OFF + BR):
                    p = turn(fp[k, t + 1, r : r + step], -(SLOT * s + HALF))
                    fa[k + 1, l + 1, r : r + step] = image_a(p, k, l + 1, r, step)[1]
                return carry

            def tile(i, carry):
                t = top_tile * i
                for r, n in segments(LO, HI):
                    own = [fa[k, PER * t + s + 1, r : r + n] for s in range(PER)]
                    fp[k + 1, t + 1, r : r + n] = image_p(own, k, t, r, n)
                return carry

            third = k == LOAD + 2
            lax.fori_loop(jnp.where(third, 2, 0), 5, layer, 0)
            lax.fori_loop(jnp.where(third, 1, 0), 2, tile, 0)
            return carry

        lax.fori_loop(LOAD, LOAD + 3, again, 0)

    def side_pairs():
        def mask(k, carry):
            fa[PAIRS, k, NLO:OFF] = fa[PAIRS, k, NLO:OFF] * top_ok
            fa[PAIRS, k, OFF + BR : NHI] = fa[PAIRS, k, OFF + BR : NHI] * bot_ok
            return carry

        lax.fori_loop(4, 8, mask, 0)

        def beside(u, carry):
            for r, n in segments(NLO, NHI):
                rows = slice(r, r + n)
                ok = row_ok_of(r)
                ok = lane_ok[:n] if ok is None else lane_ok[:n] * ok
                x = jnp.where(lane16[:n] >= BC - UNIT, turn(ml[3, rows], BC - UNIT - UNIT * u), 0.0)
                x = jnp.where(lane16[:n] < UNIT, turn(mr[3, rows], -UNIT * u), x)
                cb[u, rows] = jnp.where(u < 4, x, x * ok)
            return carry

        lax.fori_loop(0, 8, beside, 0)

    def outer_table(c, carry):
        for r in (NLO, OFF + BR):
            ta[c, r : r + 8] = entry(fa, (PAIRS,), c, r, 8)
        for r, n in inner:
            tb[c, r : r + n] = entry(cb, (), c, r, n)
        return carry


    def zero_sums():
        for k in range(6):
            acc[k] = z8

    def powers(k0, count, which, keep=True):
        def one(i, carry):
            j, t = which(i)
            k = k0 + j
            acc0 = acc1 = jnp.zeros((8, BC), F32)
            for r, cnt in segments(NLO, NHI) if keep else chunks(OFF, OFF + BR, step):
                p = fp[k, t + 1, r : r + cnt]
                own = []
                for s in range(PER):
                    l = PER * t + s + 1
                    a, out = image_a(turn(p, -(SLOT * s + HALF)), k, l, r, cnt)
                    own.append(a)
                    if row_ok_of(r) is None:
                        acc0 = acc0 + fold(a * a)
                        acc1 = acc1 + fold(a * out)
                    if keep:
                        fa[k + 1, l, r : r + cnt] = out
                if keep:
                    fp[k + 1, t + 1, r : r + cnt] = image_p(own, k, t, r, cnt)
            acc[2 * j] = acc[2 * j] + acc0
            acc[2 * j + 1] = acc[2 * j + 1] + acc1
            return carry

        lax.fori_loop(0, count, one, 0)

    def update(n, carry):
        k0 = LOAD + 4 * n
        if n == 0:
            zero_sums()
            powers(k0, 3 * TILES, lambda i: (lax.div(i, TILES), lax.rem(i, TILES)))
        else:
            powers(
                k0,
                2 + TILES,
                lambda i: (jnp.where(i < 2, 0, 1), jnp.where(i < 2, top_tile * i, i - 2)),
            )
            powers(k0, TILES, lambda i: (2, i), keep=False)

        row = jnp.zeros((1, BC), F32)
        for k in range(6):
            row = row + jnp.where(row_lane == k, jnp.sum(acc[k], keepdims=True), 0.0)
        mrow[n, 0] = row
        mbuf[n, me] = row

        def go(i, carry):
            pltpu.make_async_remote_copy(
                mrow.at[n, 0], mbuf.at[n, me], as_.at[n], ar.at[n], device_id=peer(i), device_id_type=MESH
            ).start()
            return carry

        lax.fori_loop(0, NPEER - 1, go, 0)

        send_early(n)
        when(n == 0)(far_tier)
        send_rest(n)
        when(n == 0)(side_pairs)

        pltpu.make_async_copy(others(n), others(n), ar.at[n]).wait()
        total = jnp.sum(mbuf[n], axis=0)
        mz[n, 2] = total
        for c in relays(n):
            c.start()
        coefficients(total, n)

        @when(n == 0)
        def _():
            def residual(t, carry):
                c = [co[0, k] for k in range(3)]
                g = [1.0 - SHIFT * c[0], -(c[0] + SHIFT * c[1]), -(c[1] + SHIFT * c[2]), -c[2]]
                for r, cnt in inner:
                    rows = slice(r, r + cnt)
                    for ref, l in [(fp, t + 1)] + [(fa, PER * t + s + 1) for s in range(PER)]:
                        x = [g[k][:cnt] * ref[LOAD + k, l, rows] for k in range(4)]
                        ref[LOAD + 4, l, rows] = (x[0] + x[1]) + (x[2] + x[3])
                return carry

            lax.fori_loop(0, TILES, residual, 0)
            lax.fori_loop(0, SPAN * SPAN, outer_table, 0)

        @when(n == 1)
        def _():
            def answer(l, carry):
                for r, cnt in chunks(OFF, OFF + BR, step):
                    x = combine(fa, LOAD, 0, l, r, cnt) + combine(fa, LOAD + 4, 1, l, r, cnt)
                    sol[l - 1, r - OFF : r - OFF + cnt] = x
                return carry

            lax.fori_loop(1, CZ + 1, answer, 0)

        for r, cnt in chunks(LO, HI, step):
            face[0, r : r + cnt] = combine(fa, k0, n, CZ, r, cnt)
            side_face[0, r : r + cnt] = turn(combine(fp, k0, n, TILES, r, cnt), HALF)

        for (r, cnt), x, y in zip(inner, *pull(0)):
            face[0, r : r + cnt] = x
            side_face[0, r : r + cnt] = y
        if n == 0:
            zero_sums()
            powers(LOAD + 4, TILES - 2, lambda i: (0, i + 1))

        for c in relays(n) + faces(n, range(5)):
            c.wait_recv()

        def solve(side, carry):
            coefficients(mz[n, side], 2 + side)
            return carry

        lax.fori_loop(0, 2, solve, 0)

        def from_body(side, where, r, cnt):
            at = slice(r - NLO, r - NLO + cnt)
            c = [co[where, k][:cnt] for k in range(3)]
            x = [c[k] * got[n, side, k, at] for k in range(3)]
            packed = got[n, side, 3, at]
            y = [c[k] * turn(packed, -(SLOT * k + HALF)) for k in range(3)]
            return (x[0] + x[1]) + x[2], (y[0] + y[1]) + y[2]

        for r in (LO, NHI):
            face[1, r : r + 8] = z8
            side_face[1, r : r + 8] = z8
        for r, cnt in inner:
            rows = slice(r, r + cnt)
            face[1, rows], side_face[1, rows] = from_body(1, 2, r, cnt)

        pieces = inner if n == 0 else block
        for (r, cnt), x, y in zip(pieces, *pull(1, pieces, n == 0)):
            face[1, r : r + cnt] = x
            side_face[1, r : r + cnt] = y

        for r, cnt in inner:
            rows = slice(r, r + cnt)
            x, y = from_body(0, 3, r, cnt)
            mult[0, rows] = 2.0 * mult[0, rows] + scale_up * (x - face[0, rows])
            mult[1, rows] = 2.0 * mult[1, rows] + scale_up * (y - side_face[0, rows])
            x = scale_dn * (combine(fa, k0, n, 1, r, cnt) - face[1, rows])
            low[rows] = 2.0 * low[rows] + x
        for (r, cnt), x, y in zip(pieces, *push(pieces)):
            force[0, r : r + cnt] = x
            if n == 0:
                force[1, r : r + cnt] = y

        @when(n == 0)
        def _():
            for r, cnt in segments(NLO, NHI):
                rows = slice(r, r + cnt)
                ok = row_ok_of(r)
                x, y = force[0, rows], force[1, rows] * lane_ok[:cnt]
                if ok is not None:
                    x, y = x * ok, y * ok
                fa[LOAD + 4, CZ, rows] = fa[LOAD + 4, CZ, rows] + x
                back = jnp.where(high_slot[:cnt], turn(y, -HALF), 0.0)
                fp[LOAD + 4, TILES, rows] = fp[LOAD + 4, TILES, rows] + back
                fa[LOAD + 4, 1, rows] = fa[LOAD + 4, 1, rows] - low[rows]
                y = scale_dn * (turn(combine(fp, LOAD, 0, 1, r, cnt), -HALF) - side_face[1, rows])
                back = jnp.where(low_slot[:cnt], turn(y, HALF), 0.0)
                fp[LOAD + 4, 1, rows] = fp[LOAD + 4, 1, rows] - back

        return carry

    update(0, 0)
    update(1, 0)

    for r, n in chunks(OFF, OFF + BR, step):
        ifl[CZ - 1, r - OFF : r - OFF + n] = force[0, r : r + n]
        ifl[0, r - OFF : r - OFF + n] = -low[r : r + n]
    for n in range(2):
        for c in relays(n) + faces(n, range(5)):
            c.wait_send()
    for c in near + late:
        c.wait_send()
    for n in range(2):
        pltpu.make_async_copy(others(n), others(n), as_.at[n]).wait()


def per_device(load, stiffness, pair_code, pair_weight):
    def plane(*lead):
        return pltpu.VMEM((*lead, ROWS, BC), F32)

    def vmem(*shape):
        return pltpu.VMEM((*shape, BC), F32)

    dma = pltpu.SemaphoreType.DMA
    nsend, near = 22, NHI - NLO
    scratch = [
        plane(10, CZ + 2), plane(10, TILES + 2), pltpu.VMEM((4, BR, BC), jnp.int32), plane(8),
        vmem(4, BR), vmem(4, BR), plane(4), plane(4), vmem(2, 2, CZ, 8),
        plane(SPAN * SPAN), plane(SPAN * SPAN), plane(), plane(), plane(2), plane(2), plane(2), plane(), plane(2),
        vmem(2, 4, near), vmem(2, near), vmem(2, 2, 4, near), vmem(6, 8), vmem(4, 3, 16),
        vmem(2, 1, 1), vmem(2, NPEER, 1), vmem(2, 3, 1),
        dma((4,)), dma((nsend,)), dma((nsend,)), dma((2, 5)), dma((2, 5)),
        dma((2,)), dma((2,)), dma((2, 2)), dma((2, 2)),
    ]
    return pl.pallas_call(
        kernel,
        out_shape=(pltpu.VMEM((CZ, BR, BC), F32),) * 2,
        in_specs=[pl.BlockSpec(memory_space=pl.ANY)] * 4,
        out_specs=[pl.BlockSpec(memory_space=pltpu.VMEM)] * 2,
        scratch_shapes=scratch,
        compiler_params=pltpu.CompilerParams(collective_id=0, has_side_effects=True),
        name="uzawa",
    )(load, stiffness, pair_code, pair_weight)


def solution(mesh):
    return jax.shard_map(
        per_device,
        mesh=mesh,
        in_specs=(
            P("body", "gx", "gy"),
            P("body", "gx", "gy"),
            P(None, "gx", "gy"),
            P(None, "gx", "gy"),
        ),
        out_specs=(P("body", "gx", "gy"), P("body", "gx", "gy")),
        check_vma=False,
    )
```
